32 devices in a mesh: members: 2 (over y), lat: 4 (over z), lon: 2 (over x), chan: 2 (over core).
Axes of the slice: x: 2, y: 2, z: 4, core: 2. Of those that a mesh axis runs over, the one named last changes fastest.
Arguments:
- atmos_state: float32 [768, 96, 384], P(('members', 'lon', 'chan'), 'lat'), parts along dimension 0, may hold values from -6 to 6
- ocean_state: float32 [400, 16, 512], P('members', 'lat', ('lon', 'chan')), parts along dimension 0, may hold values from -6 to 6
- land_mask: int32 [16, 512], P('lat', ('lon', 'chan')), may hold values from 0 to 1, as said below
- spectral_filter: float32 [2, 384, 384, 96], P(None, ('lon', 'chan'), 'lat'), may hold values from -6 to 6
- atmos_gain: float32 [384], P(('lon', 'chan')), may hold values from 0.1 to 1.9
- flux_readout: float32 [8, 384], P(None, ('lon', 'chan')), may hold values from -0.3125 to 0.3125
- surface_coupling: float32 [384, 4], P(('lon', 'chan')), may hold values from -3 to 3
- surface_readout: float32 [4, 200], replicated, may hold values from -0.4375 to 0.4375
- flux_coupling: float32 [200, 8], replicated, may hold values from -2 to 2
- atmos_row_source: int32 [96, 2], P('lat'), may hold values from 0 to 15, as said below
- atmos_row_weight: float32 [96, 2], P('lat'), may hold values from 0.2 to 1
- atmos_col_source: int32 [384, 2], P(('lon', 'chan')), may hold values from 0 to 511, as said below
- atmos_col_weight: float32 [384, 2], P(('lon', 'chan')), may hold values from 0.2 to 1
- ocean_row_source: int32 [16, 2], P('lat'), may hold values from 0 to 95, as said below
- ocean_row_weight: float32 [16, 2], P('lat'), may hold values from 0.2 to 1
- ocean_col_source: int32 [512, 2], P(('lon', 'chan')), may hold values from 0 to 383, as said below
- ocean_col_weight: float32 [512, 2], P(('lon', 'chan')), may hold values from 0.2 to 1
- depth_taps: float32 [2, 200, 9], replicated, may hold values from -2 to 2
- block_gain: float32 [2, 200], replicated, may hold values from 0.1 to 1.9
- expand_weight: float32 [2, 200, 800], replicated, may hold values from -0.4375 to 0.4375
- reduce_weight: float32 [2, 800, 200], replicated, may hold values from -0.21875 to 0.21875
- layer_scale: float32 [2, 200], replicated, may hold values from 0.1 to 1.9
Outputs:
- atmos_next: float32 [768, 96, 384], P(('members', 'lon', 'chan'), 'lat'), parts along dimension 0
- ocean_next: float32 [400, 16, 512], P('members', 'lat', ('lon', 'chan')), parts along dimension 0
The draws below stay inside these ranges and needn't reach their ends.
There are 2 independent parts, one for each index of `members`. The reference program is written for one: setup_inputs(seed, part) draws one part's arguments, and reference() takes and returns one part's arrays. A program takes and returns all parts, laid end to end along the dimension named above; an argument that names none is the same for every part. Nothing has to cross between parts.
Inputs may be any that keep to these rules, and one draw needn't show every extreme that they name: `atmos_row_source`: row t holds b and b + 1, where b - (16 * t) // 96 is -1, 0 or 1 before b is clipped to 0 .. 14; the offsets -1 and 1 both occur. `atmos_col_source`: row t holds b mod 512 and (b + 1) mod 512, where b - (512 * t) // 384 is -1, 0 or 1; the offsets -1 and 1 both occur. `ocean_row_source`: row t holds b and b + 1, where b - (96 * t) // 16 is -1, 0 or 1 before b is clipped to 0 .. 94; the offsets -1 and 1 both occur. `ocean_col_source`: row t holds b mod 384 and (b + 1) mod 384, where b - (384 * t) // 512 is -1, 0 or 1; the offsets -1 and 1 both occur. `land_mask`: the first and last latitude rows are land.
All inputs are finite; a program needn't handle non-finite values.
Results may differ from the reference program's by a relative error of at most 0.0001.
Values sent between devices are 32-bit elements; how exact they have to be, the bound alone decides.
A program may use at most 128 MiB of HBM per device.

```python
import jax
import jax.numpy as jnp
from jax import lax

CO = 200
HIDO = 800
CA = 384
HA = 96
WA = 384
NS = 4
NF = 8
NBLK = 2
HO = 16
WO = 512


def intersection_table(key, target, source, periodic):
    places = jnp.arange(target, dtype=jnp.int32)
    centre = places * source // target
    jitter = jax.random.randint(key, (target,), -1, 2, dtype=jnp.int32)
    middle = target // 2
    jitter = jnp.where(places == middle, -1, jnp.where(places == middle + 1, 1, jitter))
    lowest = centre + jitter
    if periodic:
        leading = jnp.mod(lowest, source)
        second = jnp.mod(lowest + 1, source)
    else:
        leading = jnp.clip(lowest, 0, source - 2)
        second = leading + 1
    return jnp.stack([leading, second], axis=1).astype(jnp.int32)


def draw_atmos_row_source(key, part):
    return intersection_table(key, HA, HO, False)


def draw_atmos_col_source(key, part):
    return intersection_table(key, WA, WO, True)


def draw_ocean_row_source(key, part):
    return intersection_table(key, HO, HA, False)


def draw_ocean_col_source(key, part):
    return intersection_table(key, WO, WA, True)


def draw_land_mask(key, part):
    cells = jax.random.randint(key, (HO, WO), 0, 4, dtype=jnp.int32)
    watery = (cells > 0).astype(jnp.int32)
    row_ids = jnp.arange(HO, dtype=jnp.int32)[:, None]
    return jnp.where((row_ids == 0) | (row_ids == HO - 1), 0, watery).astype(jnp.int32)


def block_scale(own_key, shape, cuts, low, top_value):
    def one(dim, shards_of):
        heights = jax.random.uniform(jax.random.fold_in(jax.random.fold_in(own_key, 6), dim), (shards_of,), jnp.float32, low / len(cuts), top_value / len(cuts))
        return jnp.repeat(jnp.exp(heights), shape[dim] // shards_of).reshape((-1,) + (1,) * (len(shape) - dim - 1))

    factor_of = one(*cuts[0])
    for cut in cuts[1:]:
        factor_of = factor_of * one(*cut)
    return factor_of


def normal_values(key, dims, scale, limit, shards=(), held_as=jnp.bfloat16):
    array = jax.random.normal(key, dims, jnp.float32) * scale
    if len(shards) > 0:
        array = block_scale(key, dims, shards, -0.22, 0.18) * array
    return jnp.clip(array, min=-limit, max=limit).astype(held_as)


def setup_inputs(seed: int = 0, part: int = 0) -> dict:
    streams_of = jax.random.split(jax.random.key(seed), 23)
    own_keys = jax.random.split(jax.random.fold_in(streams_of[22], part), 23)
    return {
        "atmos_state": normal_values(own_keys[0], (CA, HA, WA), 1.0, 6.0, ((0, 4), (1, 4)), jnp.float32),
        "ocean_state": normal_values(own_keys[1], (CO, HO, WO), 1.0, 6.0, ((1, 4), (2, 4)), jnp.float32),
        "land_mask": draw_land_mask(jax.random.fold_in(streams_of[22], 71), part),
        "spectral_filter": normal_values(streams_of[3], (2, CA, WA, HA), 1.0, 6.0, ((1, 4), (2, 4)), jnp.float32),
        "atmos_gain": jnp.clip(1.0 + 0.18 * jax.random.normal(streams_of[4], (CA,), jnp.float32), 0.1, 1.9),
        "flux_readout": normal_values(streams_of[5], (NF, CA), CA ** -0.5, 0.3125, ((1, 4),), jnp.float32),
        "surface_coupling": normal_values(streams_of[6], (CA, NS), NS ** -0.5, 3.0, ((0, 4),), jnp.float32),
        "surface_readout": normal_values(streams_of[7], (NS, CO), CO ** -0.5, 0.4375, (), jnp.float32),
        "flux_coupling": normal_values(streams_of[8], (CO, NF), NF ** -0.5, 2.0, (), jnp.float32),
        "atmos_row_source": draw_atmos_row_source(jax.random.fold_in(streams_of[22], 71), part),
        "atmos_row_weight": jnp.clip(0.2 + 0.8 * jax.random.uniform(streams_of[10], (HA, 2), jnp.float32) ** block_scale(streams_of[10], (HA, 2), ((0, 4),), -0.2, 0.2), 0.2, 1.0),
        "atmos_col_source": draw_atmos_col_source(jax.random.fold_in(streams_of[22], 71), part),
        "atmos_col_weight": jnp.clip(0.2 + 0.8 * jax.random.uniform(streams_of[12], (WA, 2), jnp.float32) ** block_scale(streams_of[12], (WA, 2), ((0, 4),), -0.2, 0.2), 0.2, 1.0),
        "ocean_row_source": draw_ocean_row_source(jax.random.fold_in(streams_of[22], 71), part),
        "ocean_row_weight": jnp.clip(0.2 + 0.8 * jax.random.uniform(streams_of[14], (HO, 2), jnp.float32) ** block_scale(streams_of[14], (HO, 2), ((0, 4),), -0.2, 0.2), 0.2, 1.0),
        "ocean_col_source": draw_ocean_col_source(jax.random.fold_in(streams_of[22], 71), part),
        "ocean_col_weight": jnp.clip(0.2 + 0.8 * jax.random.uniform(streams_of[16], (WO, 2), jnp.float32) ** block_scale(streams_of[16], (WO, 2), ((0, 4),), -0.2, 0.2), 0.2, 1.0),
        "depth_taps": normal_values(streams_of[17], (NBLK, CO, 9), 9 ** -0.5, 2.0, (), jnp.float32),
        "block_gain": jnp.clip(1.0 + 0.18 * jax.random.normal(streams_of[18], (NBLK, CO), jnp.float32), 0.1, 1.9),
        "expand_weight": normal_values(streams_of[19], (NBLK, CO, HIDO), CO ** -0.5, 0.4375, (), jnp.float32),
        "reduce_weight": normal_values(streams_of[20], (NBLK, HIDO, CO), HIDO ** -0.5, 0.21875, (), jnp.float32),
        "layer_scale": jnp.clip(1.0 + 0.18 * jax.random.normal(streams_of[21], (NBLK, CO), jnp.float32), 0.1, 1.9),
    }


EPSILON = 1e-05
PRECISE = lax.Precision.HIGHEST

def shares_of(weight):
    return weight / lax.optimization_barrier(jnp.sum(weight, axis=1, keepdims=True))

def regrid(field, row_source, row_weight, col_source, col_weight):
    row_share = shares_of(row_weight)
    col_share = shares_of(col_weight)
    by_rows = field[:, row_source[:, 0], :] * row_share[None, :, 0:1] + field[:, row_source[:, 1], :] * row_share[None, :, 1:2]
    return by_rows[:, :, col_source[:, 0]] * col_share[None, None, :, 0] + by_rows[:, :, col_source[:, 1]] * col_share[None, None, :, 1]

def depthwise(field, taps):
    height = field.shape[1]
    width = field.shape[2]
    padded = jnp.pad(field, ((0, 0), (1, 1), (0, 0)))
    padded = jnp.concatenate([padded[:, :, -1:], padded, padded[:, :, :1]], axis=2)
    result = jnp.zeros_like(field)
    for row_off in range(3):
        for col_off in range(3):
            result = result + taps[:, 3 * row_off + col_off][:, None, None] * padded[:, row_off:row_off + height, col_off:col_off + width]
    return result

def channel_mixer(values, gain, expand, reduce_w):
    centre = lax.optimization_barrier(jnp.mean(values, axis=0))
    spread = lax.optimization_barrier(jnp.mean(values * values, axis=0)) - centre * centre
    normed = (values - centre) * lax.rsqrt(spread + EPSILON) * gain[:, None]
    hidden = jax.nn.gelu(jnp.einsum('cd,cp->dp', expand, normed, precision=PRECISE))
    return jnp.einsum('dc,dp->cp', reduce_w, hidden, precision=PRECISE)

def reference(atmos_state, ocean_state, land_mask, spectral_filter, atmos_gain, flux_readout, surface_coupling, surface_readout, flux_coupling, atmos_row_source, atmos_row_weight, atmos_col_source, atmos_col_weight, ocean_row_source, ocean_row_weight, ocean_col_source, ocean_col_weight, depth_taps, block_gain, expand_weight, reduce_weight, layer_scale):
    centre = lax.optimization_barrier(jnp.sum(atmos_state, axis=0)) / CA
    spread = lax.optimization_barrier(jnp.sum(atmos_state * atmos_state, axis=0)) / CA - centre * centre
    normed = (atmos_state - centre) * lax.rsqrt(spread + EPSILON) * atmos_gain[:, None, None]
    spectrum = jnp.fft.fft2(normed, axes=(1, 2))
    kernel = jnp.transpose(spectral_filter[0] + 1j * spectral_filter[1], (0, 2, 1))
    filtered = jnp.real(jnp.fft.ifft2(kernel * spectrum, axes=(1, 2)))
    surface = jnp.einsum('sc,chw->shw', surface_readout, ocean_state, precision=PRECISE)
    surface_atmos = regrid(surface, atmos_row_source, atmos_row_weight, atmos_col_source, atmos_col_weight)
    atmos_next = atmos_state + filtered + jnp.einsum('cs,shw->chw', surface_coupling, surface_atmos, precision=PRECISE)
    flux = jnp.einsum('fc,chw->fhw', flux_readout, atmos_state, precision=PRECISE)
    flux_ocean = regrid(flux, ocean_row_source, ocean_row_weight, ocean_col_source, ocean_col_weight)
    ocean_mask = land_mask.astype(jnp.float32)
    current = ocean_mask * (ocean_state + jnp.einsum('cf,fhw->chw', flux_coupling, flux_ocean, precision=PRECISE))
    for which in range(NBLK):
        conv = depthwise(current, depth_taps[which])
        by_rows = jnp.transpose(conv, (1, 0, 2))
        gain = block_gain[which]
        expand = expand_weight[which]
        reduce_w = reduce_weight[which]
        update = lax.map(lambda row_vals: channel_mixer(row_vals, gain, expand, reduce_w), by_rows)
        update = jnp.transpose(update, (1, 0, 2))
        current = ocean_mask * (current + layer_scale[which][:, None, None] * update)
    return (atmos_next, current)
```

```python
import functools
import math

import jax
import jax.numpy as jnp
from jax import lax
from jax.experimental import pallas as pl
from jax.experimental.pallas import tpu as pltpu
from jax.sharding import PartitionSpec as P

CA = 384


EPSILON = 1e-05
PRECISE = lax.Precision.HIGH
EXACT = lax.Precision.HIGHEST
LANES = 128
PACK = 4
TABLE_ROWS = 16


def padded(x, sides, width):
    for axis, dim in sides:
        count, length = (lax.axis_size(axis), x.shape[dim])
        up = [(i, (i + 1) % count) for i in range(count)]
        down = [(j, i) for i, j in up]
        last = lax.slice_in_dim(x, length - width, length, axis=dim)
        leading = lax.slice_in_dim(x, 0, width, axis=dim)
        before = lax.ppermute(last, axis, up)
        after = lax.ppermute(leading, axis, down)
        x = jnp.concatenate([before, x, after], axis=dim)
    return x


def fourier_tables(length):
    places = jnp.arange(length, dtype=jnp.int32)
    angles = (
        2.0
        * math.pi
        / length
        * jnp.mod(places[:, None] * places[None, :], length).astype(jnp.float32)
    )
    return (jnp.cos(angles), jnp.sin(angles))


def regrid_matrix(source, weight, offset, span, period):
    shares = weight / jnp.sum(weight, axis=1, keepdims=True)
    relative = source - offset
    if period > 0:
        relative = jnp.mod(relative, period)
    columns = jnp.arange(span, dtype=relative.dtype)[None, :]
    return shares[:, 0:1] * (relative[:, 0:1] == columns).astype(jnp.float32) + shares[:, 1:2] * (
        relative[:, 1:2] == columns
    ).astype(jnp.float32)


def apply_maps(field, row_map, col_map):
    by_rows = jnp.einsum("jh,shw->sjw", row_map, field, precision=PRECISE)
    return jnp.einsum("sjw,kw->sjk", by_rows, col_map, precision=PRECISE)


def grid_rims(field):
    return padded(field, (("lat", 1), (("lon", "chan"), 2)), 2)


def along_last(field, table):
    return jnp.einsum("ckh,hm->ckm", field, table, precision=PRECISE)


def global_filter(normed, spectral_filter):
    width_len = normed.shape[2]
    height_len = spectral_filter.shape[3]
    cos_w, sin_w = fourier_tables(width_len)
    cos_h, sin_h = fourier_tables(height_len)
    real_w = jnp.einsum("chn,nk->ckh", normed, cos_w, precision=PRECISE)
    imag_w = -jnp.einsum("chn,nk->ckh", normed, sin_w, precision=PRECISE)
    real_w, imag_w = (
        lax.all_to_all(real_w, "lat", split_axis=1, concat_axis=2, tiled=True),
        lax.all_to_all(imag_w, "lat", split_axis=1, concat_axis=2, tiled=True),
    )
    real_s = along_last(real_w, cos_h) + along_last(imag_w, sin_h)
    imag_s = along_last(imag_w, cos_h) - along_last(real_w, sin_h)
    kern_real = spectral_filter[0]
    kern_imag = spectral_filter[1]
    real_f = kern_real * real_s - kern_imag * imag_s
    imag_f = kern_real * imag_s + kern_imag * real_s
    real_b = (along_last(real_f, cos_h) - along_last(imag_f, sin_h)) / height_len
    imag_b = (along_last(imag_f, cos_h) + along_last(real_f, sin_h)) / height_len
    real_b, imag_b = (
        lax.all_to_all(real_b, "lat", split_axis=2, concat_axis=1, tiled=True),
        lax.all_to_all(imag_b, "lat", split_axis=2, concat_axis=1, tiled=True),
    )
    back = jnp.einsum("ckh,kn->chn", real_b, cos_w, precision=PRECISE) - jnp.einsum(
        "ckh,kn->chn", imag_b, sin_w, precision=PRECISE
    )
    return back / width_len


def split_value(x):
    high = x.astype(jnp.bfloat16)
    return high, (x - high.astype(jnp.float32)).astype(jnp.bfloat16)


def wave(rows, columns, length):
    steps = lax.rem(rows * columns, length)
    angles = (2.0 * math.pi / length) * steps.astype(jnp.float32)
    return jnp.cos(angles), jnp.sin(angles)


def fill_tables(w_hi, w_lo, f_hi, f_lo, b_hi, b_lo):
    width, height = w_hi.shape[0], f_hi.shape[0] // 2

    def places(block, columns):
        shape = (TABLE_ROWS, columns)
        rows = lax.broadcasted_iota(jnp.int32, shape, 0) + block * TABLE_ROWS
        return rows, lax.broadcasted_iota(jnp.int32, shape, 1)

    def span(block):
        return pl.ds(pl.multiple_of(block * TABLE_ROWS, TABLE_ROWS), TABLE_ROWS)

    def along_width(block, carry):
        cos_w, sin_w = wave(*places(block, width), width)
        w_hi[span(block), :width], w_lo[span(block), :width] = split_value(cos_w)
        w_hi[span(block), width:], w_lo[span(block), width:] = split_value(-sin_w)
        return carry

    def along_height(block, carry):
        rows, columns = places(block, 2 * height)
        lower, right = rows >= height, columns >= height
        cos_h, sin_h = wave(
            jnp.where(lower, rows - height, rows), jnp.where(right, columns - height, columns), height
        )
        level = lower == right
        forward = jnp.where(level, cos_h, jnp.where(right, sin_h, -sin_h))
        inverse = jnp.where(level, cos_h, jnp.where(right, -sin_h, sin_h)) / (height * width)
        f_hi[span(block), :], f_lo[span(block), :] = split_value(forward)
        b_hi[span(block), :], b_lo[span(block), :] = split_value(inverse)
        return carry

    lax.fori_loop(0, width // TABLE_ROWS, along_width, 0)
    lax.fori_loop(0, 2 * height // TABLE_ROWS, along_height, 0)


def product(left, right):
    dot = functools.partial(jnp.dot, preferred_element_type=jnp.float32)
    return dot(left[0], right[0]) + (dot(left[0], right[1]) + dot(left[1], right[0]))


def pack_kernel(member_ref, filter_ref, packed_ref):
    del member_ref
    piece = LANES // PACK
    for part in range(filter_ref.shape[0]):
        last = filter_ref[part, 0, 0, 0, PACK - 1]
        for j in range(PACK - 1):
            packed_ref[0, part, 0, j] = jnp.concatenate(
                [filter_ref[part, 0, 0, 0, j], last[:, piece * j : piece * (j + 1)]],
                axis=1,
            )


def pack_filter(spectral_filter, lat_count, members, first, count):
    parts, channels, freqs, height_len = spectral_filter.shape
    groups = channels // (lat_count * members * PACK)
    member = lax.axis_index("members").astype(jnp.int32).reshape(1)
    split = spectral_filter.reshape(parts, lat_count, members, groups, PACK, freqs, height_len)
    return pl.pallas_call(
        pack_kernel,
        out_shape=jax.ShapeDtypeStruct(
            (lat_count, parts, count, PACK - 1, freqs, LANES), jnp.float32
        ),
        grid_spec=pltpu.PrefetchScalarGridSpec(
            num_scalar_prefetch=1,
            grid=(lat_count, count),
            in_specs=[
                pl.BlockSpec(
                    (parts, 1, 1, 1, PACK, freqs, height_len),
                    lambda i, g, m: (0, i, m[0], g + first, 0, 0, 0),
                )
            ],
            out_specs=pl.BlockSpec(
                (1, parts, 1, PACK - 1, freqs, LANES), lambda i, g, m: (i, 0, g, 0, 0, 0)
            ),
        ),
        cost_estimate=pl.CostEstimate(
            flops=0,
            transcendentals=0,
            bytes_accessed=6 * spectral_filter.size * count // groups,
        ),
    )(member, split)


def filter_group(x_ref, filter_ref, tables, out_ref, wide_ref):
    blocks, _, block_rows, width = x_ref.shape
    height = blocks * block_rows
    w_hi, w_lo, f_hi, f_lo, b_hi, b_lo = tables
    table_w = (w_hi[...], w_lo[...])
    forward = (f_hi[...], f_lo[...])
    inverse = (b_hi[...], b_lo[...])
    rows = jnp.concatenate([x_ref[:, j].reshape(height, width) for j in range(PACK)], axis=0)
    spectra = product(split_value(rows), table_w)
    packed = [
        [filter_ref[:, part, j].reshape(width, LANES).T for j in range(PACK - 1)]
        for part in range(2)
    ]
    kernels = [
        [p[:height] for p in of_part] + [jnp.concatenate([p[height:] for p in of_part], axis=0)]
        for of_part in packed
    ]
    for j in range(PACK):
        own = spectra[height * j : height * (j + 1)]
        stacked = jnp.concatenate([own[:, :width], own[:, width:]], axis=0)
        full = product(forward, split_value(stacked))
        real_s, imag_s = full[:height], full[height:]
        real_k, imag_k = kernels[0][j], kernels[1][j]
        filtered = jnp.concatenate(
            [real_k * real_s - imag_k * imag_s, real_k * imag_s + imag_k * real_s], axis=0
        )
        back = product(inverse, split_value(filtered))
        wide_ref[height * j : height * (j + 1), :width] = back[:height]
        wide_ref[height * j : height * (j + 1), width:] = back[height:]
    wide = split_value(wide_ref[...])
    result = product(
        (wide[0][:, :width], wide[1][:, :width]), (table_w[0][:, :width], table_w[1][:, :width])
    ) + product(
        (wide[0][:, width:], wide[1][:, width:]), (table_w[0][:, width:], table_w[1][:, width:])
    )
    for j in range(PACK):
        own = result[height * j : height * (j + 1)]
        out_ref[:, j] = own.reshape(blocks, block_rows, width)


def spectral_kernel(
    normed_ref, first_ref, rest_ref, out_ref,
    kernels_ref, arrived_ref, back_ref, wide_ref, w_hi, w_lo, f_hi, f_lo, b_hi, b_lo,
    go_send, go_recv, go_local, come_send, come_recv, come_local, swap_send, swap_recv, own_sem,
):
    count = normed_ref.shape[0]
    steps = arrived_ref.shape[0]
    groups = steps // 2
    me = lax.axis_index("lat")
    member = lax.axis_index("members")
    peers = [(k, lax.rem(me + k, count)) for k in range(1, count)]
    barrier = pltpu.get_barrier_semaphore()
    for _, peer in peers:
        pl.semaphore_signal(
            barrier, inc=1, device_id={"lat": peer}, device_id_type=pl.DeviceIdType.MESH
        )
    pl.semaphore_signal(
        barrier, inc=1, device_id={"members": 1 - member}, device_id_type=pl.DeviceIdType.MESH
    )

    def place(step):
        second = step // groups
        return member + second - 2 * member * second, pl.ds(PACK * (step % groups), PACK)

    def going(step, k, peer):
        half, span = place(step)
        return pltpu.make_async_remote_copy(
            src_ref=normed_ref.at[peer, half, span],
            dst_ref=arrived_ref.at[step, me],
            send_sem=go_send.at[step, k - 1],
            recv_sem=go_recv.at[step, k - 1],
            device_id={"lat": peer},
            device_id_type=pl.DeviceIdType.MESH,
        )

    def staying(step):
        half, span = place(step)
        return pltpu.make_async_copy(
            normed_ref.at[me, half, span], arrived_ref.at[step, me], go_local.at[step]
        )

    def coming(step, k, peer):
        half, span = place(step)
        return pltpu.make_async_remote_copy(
            src_ref=back_ref.at[step, peer],
            dst_ref=out_ref.at[me, half, span],
            send_sem=come_send.at[step, k - 1],
            recv_sem=come_recv.at[step, k - 1],
            device_id={"lat": peer},
            device_id_type=pl.DeviceIdType.MESH,
        )

    def kept(step):
        half, span = place(step)
        return pltpu.make_async_copy(
            back_ref.at[step, me], out_ref.at[me, half, span], come_local.at[step]
        )

    def held(group):
        begun = first_ref.shape[2]
        return first_ref.at[:, :, group] if group < begun else rest_ref.at[:, :, group - begun]

    def own_filter(group):
        return pltpu.make_async_copy(held(group), kernels_ref.at[group], own_sem.at[group])

    def swapped(group):
        return pltpu.make_async_remote_copy(
            src_ref=held(group),
            dst_ref=kernels_ref.at[groups + group],
            send_sem=swap_send.at[group],
            recv_sem=swap_recv.at[group],
            device_id={"members": 1 - member},
            device_id_type=pl.DeviceIdType.MESH,
        )

    pl.semaphore_wait(barrier, count)
    for step in range(steps):
        for k, peer in peers:
            going(step, k, peer).start()
        staying(step).start()
        if step < groups:
            own_filter(step).start()
            swapped(step).start()

    fill_tables(w_hi, w_lo, f_hi, f_lo, b_hi, b_lo)

    def one_step(step, carry):
        staying(step).wait()
        for k, peer in peers:
            going(step, k, peer).wait_recv()

        for group in range(groups):

            @pl.when(step == group)
            def _():
                own_filter(group).wait()

            @pl.when(step == groups + group)
            def _():
                swapped(group).wait_recv()

        filter_group(
            arrived_ref.at[step],
            kernels_ref.at[step],
            (w_hi, w_lo, f_hi, f_lo, b_hi, b_lo),
            back_ref.at[step],
            wide_ref,
        )
        for k, peer in peers:
            coming(step, k, peer).start()
        kept(step).start()
        return carry

    lax.fori_loop(0, steps, one_step, 0)
    for group in range(groups):
        swapped(group).wait_send()
    for step in range(steps):
        kept(step).wait()
        for k, peer in peers:
            going(step, k, peer).wait_send()
            coming(step, k, peer).wait()


def spectral_step(normed, first, rest):
    lat_count, halves, _, rows, width = normed.shape
    parts, groups = first.shape[1], first.shape[2] + rest.shape[2]
    height = lat_count * rows
    steps = halves * groups
    anywhere = pl.BlockSpec(memory_space=pl.ANY)
    dma = pltpu.SemaphoreType.DMA
    tables = [(width, 2 * width)] * 2 + [(2 * height, 2 * height)] * 4
    return pl.pallas_call(
        spectral_kernel,
        out_shape=jax.ShapeDtypeStruct(normed.shape, jnp.float32),
        in_specs=[anywhere] * 3,
        out_specs=anywhere,
        scratch_shapes=[
            pltpu.VMEM((steps, lat_count, parts) + first.shape[3:], jnp.float32),
            pltpu.VMEM((steps, lat_count, PACK, rows, width), jnp.float32),
            pltpu.VMEM((steps, lat_count, PACK, rows, width), jnp.float32),
            pltpu.VMEM((PACK * height, 2 * width), jnp.float32),
            *(pltpu.VMEM(shape, jnp.bfloat16) for shape in tables),
            dma((steps, lat_count - 1)),
            dma((steps, lat_count - 1)),
            dma((steps,)),
            dma((steps, lat_count - 1)),
            dma((steps, lat_count - 1)),
            dma((steps,)),
            dma((groups,)),
            dma((groups,)),
            dma((groups,)),
        ],
        compiler_params=pltpu.CompilerParams(collective_id=1, has_side_effects=True),
        cost_estimate=pl.CostEstimate(
            flops=12 * steps * PACK * height * width * (2 * width + 2 * height),
            transcendentals=0,
            bytes_accessed=8 * normed.size + 4 * (first.size + rest.size),
        ),
    )(normed, first, rest)


def exchanged(x):
    return lax.all_to_all(x, "lat", split_axis=0, concat_axis=0, tiled=True)


def summed(x, axes):
    for axis in axes:
        if lax.axis_size(axis) == 2:
            x = x + lax.ppermute(x, axis, [(0, 1), (1, 0)])
        else:
            x = lax.psum(x, axis)
    return x


def channels_divide(atmos_state, spectral_filter, ocean_rows, ocean_cols):
    channels, rows, width = atmos_state.shape
    height = spectral_filter.shape[3]
    unit = lax.axis_size("lat") * lax.axis_size("members") * PACK
    return (
        channels % unit == 0
        and lax.axis_size("members") == 2
        and rows % 8 == 0
        and width % LANES == 0
        and PACK * height == (PACK - 1) * LANES
        and spectral_filter.shape[2] % 8 == 0
        and (lax.axis_size("lat") * rows) % TABLE_ROWS == 0
        and width % TABLE_ROWS == 0
        and channels > unit
        and width >= ocean_cols
        and rows % ocean_rows == 0
        and ocean_rows >= 4
        and rows // ocean_rows >= 3
    )


def depthwise(field, taps):
    height = field.shape[1] - 2
    width = field.shape[2] - 2
    result = jnp.zeros((field.shape[0], height, width), jnp.float32)
    for row_off in range(3):
        for col_off in range(3):
            result = (
                result
                + taps[:, 3 * row_off + col_off][:, None, None]
                * field[:, row_off : row_off + height, col_off : col_off + width]
            )
    return result


def ocean_mixer(values, gain, expand, reduce_w):
    channels, height, width = values.shape
    flat = values.reshape(channels, height * width)
    centre = jnp.mean(flat, axis=0)
    spread = jnp.mean(flat * flat, axis=0) - centre * centre
    normed = (flat - centre) * lax.rsqrt(spread + EPSILON) * gain[:, None]
    hidden = jax.nn.gelu(jnp.einsum("cd,cp->dp", expand, normed, precision=PRECISE))
    update = jnp.einsum("dc,dp->cp", reduce_w, hidden, precision=PRECISE)
    return update.reshape(channels, height, width)


def by_frequencies(
    atmos_state,
    ocean_state,
    land_mask,
    spectral_filter,
    atmos_gain,
    flux_readout,
    surface_coupling,
    surface_readout,
    flux_coupling,
    to_atmos,
    to_ocean,
    depth_taps,
    block_gain,
    expand_weight,
    reduce_weight,
    layer_scale,
):
    atmos_row_source, atmos_row_weight, atmos_col_source, atmos_col_weight = to_atmos
    ocean_row_source, ocean_row_weight, ocean_col_source, ocean_col_weight = to_ocean
    atm_rows = atmos_state.shape[1]
    width_atm = atmos_state.shape[2]
    ocean_rows = ocean_state.shape[1]
    ocean_cols = ocean_state.shape[2]
    col_groups = lax.axis_size(("lon", "chan"))
    atm_cols = width_atm // col_groups
    lat_place = lax.axis_index("lat")
    col_place = lax.axis_index(("lon", "chan"))
    partial_flux = jnp.einsum("fc,chw->fhw", flux_readout, atmos_state, precision=PRECISE)
    flux_full, column_sum, square_sum = lax.psum(
        (partial_flux, jnp.sum(atmos_state, axis=0), jnp.sum(atmos_state * atmos_state, axis=0)),
        ("lon", "chan"),
    )
    centre = column_sum / CA
    spread = square_sum / CA - centre * centre
    scale = lax.rsqrt(spread + EPSILON)
    normed = (atmos_state - centre) * scale * atmos_gain[:, None, None]
    filtered = global_filter(normed, spectral_filter)
    surface = jnp.einsum("sc,chw->shw", surface_readout, ocean_state, precision=PRECISE)
    surface_rim = grid_rims(surface)
    row_map = regrid_matrix(
        atmos_row_source, atmos_row_weight, lat_place * ocean_rows - 2, ocean_rows + 4, 0
    )
    col_map = regrid_matrix(
        atmos_col_source,
        atmos_col_weight,
        col_place * ocean_cols - 2,
        ocean_cols + 4,
        ocean_cols * col_groups,
    )
    atmos_piece = apply_maps(surface_rim, row_map, col_map)
    forcing = jnp.einsum(
        "cs,shw->chw",
        surface_coupling,
        lax.all_gather(atmos_piece, ("lon", "chan"), axis=2, tiled=True),
        precision=PRECISE,
    )
    atmos_next = atmos_state + filtered + forcing
    flux_cols = lax.dynamic_slice_in_dim(flux_full, col_place * atm_cols, atm_cols, 2)
    flux_rim = grid_rims(flux_cols)
    row_back = regrid_matrix(
        ocean_row_source, ocean_row_weight, lat_place * atm_rows - 2, atm_rows + 4, 0
    )
    col_back = regrid_matrix(
        ocean_col_source, ocean_col_weight, col_place * atm_cols - 2, atm_cols + 4, width_atm
    )
    flux_ocean = apply_maps(flux_rim, row_back, col_back)
    ocean_mask = land_mask.astype(jnp.float32)
    current = ocean_mask * (
        ocean_state + jnp.einsum("cf,fhw->chw", flux_coupling, flux_ocean, precision=PRECISE)
    )
    padded_field = grid_rims(current)
    mask_padded = grid_rims(ocean_mask[None])[0]
    update = ocean_mixer(
        depthwise(padded_field, depth_taps[0]), block_gain[0], expand_weight[0], reduce_weight[0]
    )
    widened = mask_padded[1:-1, 1:-1] * (
        padded_field[:, 1:-1, 1:-1] + layer_scale[0][:, None, None] * update
    )
    update = ocean_mixer(
        depthwise(widened, depth_taps[1]), block_gain[1], expand_weight[1], reduce_weight[1]
    )
    current = ocean_mask * (widened[:, 1:-1, 1:-1] + layer_scale[1][:, None, None] * update)
    return (atmos_next, current)


def by_channels(
    atmos_state,
    ocean_state,
    land_mask,
    spectral_filter,
    atmos_gain,
    flux_readout,
    surface_coupling,
    surface_readout,
    flux_coupling,
    to_atmos,
    to_ocean,
    depth_taps,
    block_gain,
    expand_weight,
    reduce_weight,
    layer_scale,
):
    channels, atm_rows, width_atm = atmos_state.shape
    ocean_channels, ocean_rows, ocean_cols = ocean_state.shape
    fields = surface_readout.shape[0]
    fluxes = flux_readout.shape[0]
    col_groups = lax.axis_size(("lon", "chan"))
    atm_cols = width_atm // col_groups
    lat_count = lax.axis_size("lat")
    lat_place = lax.axis_index("lat")
    col_place = lax.axis_index(("lon", "chan"))
    hold = lax.optimization_barrier

    mask = land_mask.astype(jnp.float32)
    groups = channels // (lat_count * 2 * PACK)
    packed_first = pack_filter(spectral_filter, lat_count, 2, 0, 1)
    packed_first, ocean_state, atmos_state = hold((packed_first, ocean_state, atmos_state))
    kernels_first = exchanged(packed_first)
    packed_rest = pack_filter(spectral_filter, lat_count, 2, 1, groups - 1)
    up = [(i, (i + 1) % lat_count) for i in range(lat_count)]
    down = [(j, i) for i, j in up]
    partial_flux = jnp.einsum("fc,chw->fhw", flux_readout, atmos_state, precision=EXACT)
    own_rows = regrid_matrix(to_ocean[0], to_ocean[1], lat_place * atm_rows - 1, atm_rows + 1, 0)
    by_rows = jnp.einsum("jh,fhw->fjw", own_rows[:, 1:], partial_flux, precision=PRECISE)
    weight_up = own_rows[0, 0]
    closing = partial_flux[:, -1:]

    def with_mask(rows, edge):
        edge = jnp.pad(edge, ((0, 1), (0, width_atm - ocean_cols)))
        return jnp.concatenate([rows, edge[None]], axis=0)

    to_below = with_mask(jnp.concatenate([by_rows[:, -2:], closing], axis=1), mask[-2:])
    to_above = with_mask(
        jnp.concatenate([by_rows[:, :2], jnp.broadcast_to(weight_up, closing.shape)], axis=1),
        mask[:2],
    )
    rows_before = lax.ppermute(ocean_state[:, -2:], "lat", up)
    rows_after = lax.ppermute(ocean_state[:, :2], "lat", down)
    from_above = lax.ppermute(to_below, "lat", up)
    from_below = lax.ppermute(to_above, "lat", down)
    kernels_rest = exchanged(packed_rest)
    mask_above, mask_below = from_above[fluxes, :2, :ocean_cols], from_below[fluxes, :2, :ocean_cols]
    from_above, from_below = from_above[:fluxes], from_below[:fluxes]

    flux_rows = jnp.concatenate(
        [
            from_above[:, :2],
            by_rows[:, :1] + weight_up * from_above[:, 2:],
            by_rows[:, 1:],
            from_below[:, :1] + from_below[:, 2:] * closing,
            from_below[:, 1:2],
        ],
        axis=1,
    )
    sums = jnp.stack([jnp.sum(atmos_state, axis=0), jnp.sum(atmos_state * atmos_state, axis=0)])
    ext_rows = flux_rows.shape[1]
    sent = jnp.concatenate(
        [flux_rows.reshape(fluxes * ext_rows, width_atm), sums.reshape(2 * atm_rows, width_atm)],
        axis=0,
    )
    full = summed(sent, ("chan", "lon"))
    flux_full = full[: fluxes * ext_rows].reshape(fluxes, ext_rows, width_atm)
    sums_full = full[fluxes * ext_rows :].reshape(2, atm_rows, width_atm)
    centre = sums_full[0] / CA
    spread = sums_full[1] / CA - centre * centre
    scale = lax.rsqrt(spread + EPSILON)
    normed = (atmos_state - centre) * scale * atmos_gain[:, None, None]
    own = channels // (2 * lat_count)
    halves = (lat_count, 2, own)
    normed = normed.reshape(halves + (atm_rows, width_atm))

    columns = jnp.concatenate([to_ocean[2].astype(jnp.float32), to_ocean[3]], axis=1).T
    columns = jnp.pad(columns, ((0, ocean_rows), (0, 0)))[None]
    state_rows = jnp.concatenate(
        [
            jnp.concatenate([rows_before, ocean_state, rows_after], axis=1),
            jnp.concatenate([mask_above, mask, mask_below], axis=0)[None],
            columns,
        ],
        axis=0,
    )
    state_rim = padded(state_rows, ((("lon", "chan"), 2),), 2)
    surface_rim = jnp.einsum(
        "sc,chw->shw", surface_readout, state_rim[:ocean_channels], precision=EXACT
    )
    row_map = regrid_matrix(
        to_atmos[0], to_atmos[1], lat_place * ocean_rows - 2, ocean_rows + 4, 0
    )
    col_map = regrid_matrix(
        to_atmos[2],
        to_atmos[3],
        col_place * ocean_cols - 2,
        ocean_cols + 4,
        ocean_cols * col_groups,
    )
    atmos_piece = apply_maps(surface_rim, row_map, col_map)
    spread_piece = lax.dynamic_update_slice_in_dim(
        jnp.zeros((fields, atm_rows, width_atm), jnp.float32), atmos_piece, col_place * atm_cols, 2
    )
    surface_atmos = summed(spread_piece, ("chan", "lon"))

    col_tables = state_rim[ocean_channels + 1]
    col_back = regrid_matrix(col_tables[:2].T, col_tables[2:4].T, 0.0, width_atm, 0)
    flux_ocean_rim = jnp.einsum("fhw,kw->fhk", flux_full, col_back, precision=PRECISE)

    mask_rim = state_rim[ocean_channels]
    padded_field = mask_rim * (
        state_rim[:ocean_channels]
        + jnp.einsum("cf,fhw->chw", flux_coupling, flux_ocean_rim, precision=PRECISE)
    )
    update = ocean_mixer(
        depthwise(padded_field, depth_taps[0]), block_gain[0], expand_weight[0], reduce_weight[0]
    )
    widened = mask_rim[1:-1, 1:-1] * (
        padded_field[:, 1:-1, 1:-1] + layer_scale[0][:, None, None] * update
    )
    update = ocean_mixer(
        depthwise(widened, depth_taps[1]), block_gain[1], expand_weight[1], reduce_weight[1]
    )
    ocean_next = mask * (widened[:, 1:-1, 1:-1] + layer_scale[1][:, None, None] * update)

    kernels_first, kernels_rest, normed, ocean_next, surface_atmos = hold(
        (kernels_first, kernels_rest, normed, ocean_next, surface_atmos)
    )
    filtered = spectral_step(normed, kernels_first, kernels_rest)
    by_half = atmos_state.reshape(halves + (atm_rows, width_atm))
    coupling_half = surface_coupling.reshape(halves + (fields, 1, 1))
    forcing = sum(coupling_half[:, :, :, s] * surface_atmos[s] for s in range(fields))
    atmos_next = (by_half + filtered) + forcing
    return (atmos_next.reshape(atmos_state.shape), ocean_next)


def body(
    atmos_state,
    ocean_state,
    land_mask,
    spectral_filter,
    atmos_gain,
    flux_readout,
    surface_coupling,
    surface_readout,
    flux_coupling,
    atmos_row_source,
    atmos_row_weight,
    atmos_col_source,
    atmos_col_weight,
    ocean_row_source,
    ocean_row_weight,
    ocean_col_source,
    ocean_col_weight,
    depth_taps,
    block_gain,
    expand_weight,
    reduce_weight,
    layer_scale,
):
    if channels_divide(atmos_state, spectral_filter, *ocean_state.shape[1:]):
        step = by_channels
    else:
        step = by_frequencies
    return step(
        atmos_state,
        ocean_state,
        land_mask,
        spectral_filter,
        atmos_gain,
        flux_readout,
        surface_coupling,
        surface_readout,
        flux_coupling,
        (atmos_row_source, atmos_row_weight, atmos_col_source, atmos_col_weight),
        (ocean_row_source, ocean_row_weight, ocean_col_source, ocean_col_weight),
        depth_taps,
        block_gain,
        expand_weight,
        reduce_weight,
        layer_scale,
    )


def solution(mesh):
    return jax.shard_map(
        body,
        mesh=mesh,
        in_specs=(
            P(("members", "lon", "chan"), "lat", None),
            P("members", "lat", ("lon", "chan")),
            P("lat", ("lon", "chan")),
            P(None, ("lon", "chan"), "lat", None),
            P(("lon", "chan")),
            P(None, ("lon", "chan")),
            P(("lon", "chan"), None),
            P(),
            P(),
            P("lat", None),
            P("lat", None),
            P(("lon", "chan"), None),
            P(("lon", "chan"), None),
            P("lat", None),
            P("lat", None),
            P(("lon", "chan"), None),
            P(("lon", "chan"), None),
            P(),
            P(),
            P(),
            P(),
            P(),
        ),
        out_specs=(
            P(("members", "lon", "chan"), "lat", None),
            P("members", "lat", ("lon", "chan")),
        ),
        check_vma=False,
    )
```

```python
import functools
import math

import jax
import jax.numpy as jnp
from jax import lax
from jax.experimental import pallas as pl
from jax.experimental.pallas import tpu as pltpu
from jax.sharding import PartitionSpec as P

CA = 384


EPSILON = 1e-05
PRECISE = lax.Precision.HIGH
EXACT = lax.Precision.HIGHEST
LANES = 128
PACK = 4
TABLE_ROWS = 16
RIM = 9


def padded(x, sides, width):
    for axis, dim in sides:
        count, length = (lax.axis_size(axis), x.shape[dim])
        up = [(i, (i + 1) % count) for i in range(count)]
        down = [(j, i) for i, j in up]
        last = lax.slice_in_dim(x, length - width, length, axis=dim)
        leading = lax.slice_in_dim(x, 0, width, axis=dim)
        before = lax.ppermute(last, axis, up)
        after = lax.ppermute(leading, axis, down)
        x = jnp.concatenate([before, x, after], axis=dim)
    return x


def fourier_tables(length):
    places = jnp.arange(length, dtype=jnp.int32)
    angles = (
        2.0
        * math.pi
        / length
        * jnp.mod(places[:, None] * places[None, :], length).astype(jnp.float32)
    )
    return (jnp.cos(angles), jnp.sin(angles))


def regrid_matrix(source, weight, offset, span, period):
    shares = weight / jnp.sum(weight, axis=1, keepdims=True)
    relative = source - offset
    if period > 0:
        relative = jnp.mod(relative, period)
    columns = jnp.arange(span, dtype=relative.dtype)[None, :]
    return shares[:, 0:1] * (relative[:, 0:1] == columns).astype(jnp.float32) + shares[:, 1:2] * (
        relative[:, 1:2] == columns
    ).astype(jnp.float32)


def apply_maps(field, row_map, col_map):
    by_rows = jnp.einsum("jh,shw->sjw", row_map, field, precision=PRECISE)
    return jnp.einsum("sjw,kw->sjk", by_rows, col_map, precision=PRECISE)


def grid_rims(field):
    return padded(field, (("lat", 1), (("lon", "chan"), 2)), 2)


def along_last(field, table):
    return jnp.einsum("ckh,hm->ckm", field, table, precision=PRECISE)


def global_filter(normed, spectral_filter):
    width_len = normed.shape[2]
    height_len = spectral_filter.shape[3]
    cos_w, sin_w = fourier_tables(width_len)
    cos_h, sin_h = fourier_tables(height_len)
    real_w = jnp.einsum("chn,nk->ckh", normed, cos_w, precision=PRECISE)
    imag_w = -jnp.einsum("chn,nk->ckh", normed, sin_w, precision=PRECISE)
    real_w, imag_w = (
        lax.all_to_all(real_w, "lat", split_axis=1, concat_axis=2, tiled=True),
        lax.all_to_all(imag_w, "lat", split_axis=1, concat_axis=2, tiled=True),
    )
    real_s = along_last(real_w, cos_h) + along_last(imag_w, sin_h)
    imag_s = along_last(imag_w, cos_h) - along_last(real_w, sin_h)
    kern_real = spectral_filter[0]
    kern_imag = spectral_filter[1]
    real_f = kern_real * real_s - kern_imag * imag_s
    imag_f = kern_real * imag_s + kern_imag * real_s
    real_b = (along_last(real_f, cos_h) - along_last(imag_f, sin_h)) / height_len
    imag_b = (along_last(imag_f, cos_h) + along_last(real_f, sin_h)) / height_len
    real_b, imag_b = (
        lax.all_to_all(real_b, "lat", split_axis=2, concat_axis=1, tiled=True),
        lax.all_to_all(imag_b, "lat", split_axis=2, concat_axis=1, tiled=True),
    )
    back = jnp.einsum("ckh,kn->chn", real_b, cos_w, precision=PRECISE) - jnp.einsum(
        "ckh,kn->chn", imag_b, sin_w, precision=PRECISE
    )
    return back / width_len


def split_value(x):
    high = x.astype(jnp.bfloat16)
    return high, (x - high.astype(jnp.float32)).astype(jnp.bfloat16)


def wave(rows, columns, length):
    steps = lax.rem(rows * columns, length)
    angles = (2.0 * math.pi / length) * steps.astype(jnp.float32)
    return jnp.cos(angles), jnp.sin(angles)


def fill_tables(w_hi, w_lo, f_hi, f_lo, b_hi, b_lo):
    width, height = w_hi.shape[0], f_hi.shape[0] // 2

    def places(block, columns):
        shape = (TABLE_ROWS, columns)
        rows = lax.broadcasted_iota(jnp.int32, shape, 0) + block * TABLE_ROWS
        return rows, lax.broadcasted_iota(jnp.int32, shape, 1)

    def span(block):
        return pl.ds(pl.multiple_of(block * TABLE_ROWS, TABLE_ROWS), TABLE_ROWS)

    def along_width(block, carry):
        cos_w, sin_w = wave(*places(block, width), width)
        w_hi[span(block), :width], w_lo[span(block), :width] = split_value(cos_w)
        w_hi[span(block), width:], w_lo[span(block), width:] = split_value(-sin_w)
        return carry

    def along_height(block, carry):
        rows, columns = places(block, 2 * height)
        lower, right = rows >= height, columns >= height
        cos_h, sin_h = wave(
            jnp.where(lower, rows - height, rows), jnp.where(right, columns - height, columns), height
        )
        level = lower == right
        forward = jnp.where(level, cos_h, jnp.where(right, sin_h, -sin_h))
        inverse = jnp.where(level, cos_h, jnp.where(right, -sin_h, sin_h)) / (height * width)
        f_hi[span(block), :], f_lo[span(block), :] = split_value(forward)
        b_hi[span(block), :], b_lo[span(block), :] = split_value(inverse)
        return carry

    lax.fori_loop(0, width // TABLE_ROWS, along_width, 0)
    lax.fori_loop(0, 2 * height // TABLE_ROWS, along_height, 0)


def product(left, right):
    dot = functools.partial(jnp.dot, preferred_element_type=jnp.float32)
    return dot(left[0], right[0]) + (dot(left[0], right[1]) + dot(left[1], right[0]))


def pack_kernel(member_ref, filter_ref, packed_ref):
    del member_ref
    piece = LANES // PACK
    for part in range(filter_ref.shape[0]):
        last = filter_ref[part, 0, 0, 0, PACK - 1]
        for j in range(PACK - 1):
            packed_ref[0, part, 0, j] = jnp.concatenate(
                [filter_ref[part, 0, 0, 0, j], last[:, piece * j : piece * (j + 1)]],
                axis=1,
            )


def pack_filter(spectral_filter, lat_count, members, first, count):
    parts, channels, freqs, height_len = spectral_filter.shape
    groups = channels // (lat_count * members * PACK)
    member = lax.axis_index("members").astype(jnp.int32).reshape(1)
    split = spectral_filter.reshape(parts, lat_count, members, groups, PACK, freqs, height_len)
    return pl.pallas_call(
        pack_kernel,
        out_shape=jax.ShapeDtypeStruct(
            (lat_count, parts, count, PACK - 1, freqs, LANES), jnp.float32
        ),
        grid_spec=pltpu.PrefetchScalarGridSpec(
            num_scalar_prefetch=1,
            grid=(lat_count, count),
            in_specs=[
                pl.BlockSpec(
                    (parts, 1, 1, 1, PACK, freqs, height_len),
                    lambda i, g, m: (0, i, m[0], g + first, 0, 0, 0),
                )
            ],
            out_specs=pl.BlockSpec(
                (1, parts, 1, PACK - 1, freqs, LANES), lambda i, g, m: (i, 0, g, 0, 0, 0)
            ),
        ),
        cost_estimate=pl.CostEstimate(
            flops=0,
            transcendentals=0,
            bytes_accessed=6 * spectral_filter.size * count // groups,
        ),
    )(member, split)


def filter_group(x_ref, filter_ref, tables, out_ref, wide_ref):
    blocks, _, block_rows, width = x_ref.shape
    height = blocks * block_rows
    w_hi, w_lo, f_hi, f_lo, b_hi, b_lo = tables
    table_w = (w_hi[...], w_lo[...])
    forward = (f_hi[...], f_lo[...])
    inverse = (b_hi[...], b_lo[...])
    rows = jnp.concatenate([x_ref[:, j].reshape(height, width) for j in range(PACK)], axis=0)
    spectra = product(split_value(rows), table_w)
    packed = [
        [filter_ref[:, part, j].reshape(width, LANES).T for j in range(PACK - 1)]
        for part in range(2)
    ]
    kernels = [
        [p[:height] for p in of_part] + [jnp.concatenate([p[height:] for p in of_part], axis=0)]
        for of_part in packed
    ]
    for j in range(PACK):
        own = spectra[height * j : height * (j + 1)]
        stacked = jnp.concatenate([own[:, :width], own[:, width:]], axis=0)
        full = product(forward, split_value(stacked))
        real_s, imag_s = full[:height], full[height:]
        real_k, imag_k = kernels[0][j], kernels[1][j]
        filtered = jnp.concatenate(
            [real_k * real_s - imag_k * imag_s, real_k * imag_s + imag_k * real_s], axis=0
        )
        back = product(inverse, split_value(filtered))
        wide_ref[height * j : height * (j + 1), :width] = back[:height]
        wide_ref[height * j : height * (j + 1), width:] = back[height:]
    wide = split_value(wide_ref[...])
    result = product(
        (wide[0][:, :width], wide[1][:, :width]), (table_w[0][:, :width], table_w[1][:, :width])
    ) + product(
        (wide[0][:, width:], wide[1][:, width:]), (table_w[0][:, width:], table_w[1][:, width:])
    )
    for j in range(PACK):
        own = result[height * j : height * (j + 1)]
        out_ref[:, j] = own.reshape(blocks, block_rows, width)


def ocean_block(which, source, mask_ref, taps_ref, gain_ref, scale_ref, weights, span, store):
    channels = source.shape[2]
    columns = span.stop - span.start
    expand_hi, expand_lo, reduce_hi, reduce_lo = weights

    def one_row(index, carry):
        row = index + 1 + which
        conv = jnp.zeros((columns, channels), jnp.float32)
        for row_off in range(3):
            for col_off in range(3):
                tap = 3 * row_off + col_off
                begin = span.start + col_off - 1
                conv = conv + taps_ref[which, tap : tap + 1, :] * (
                    source[row + row_off - 1, begin : begin + columns, :]
                )
        centre = jnp.sum(conv, axis=1, keepdims=True) / channels
        spread = jnp.sum(conv * conv, axis=1, keepdims=True) / channels - centre * centre
        normed = (conv - centre) * lax.rsqrt(spread + EPSILON) * gain_ref[which]
        hidden = jax.nn.gelu(product(split_value(normed), (expand_hi[...], expand_lo[...])))
        update = product(split_value(hidden), (reduce_hi[...], reduce_lo[...]))
        store(
            row,
            mask_ref[row, span, :] * (source[row, span, :] + scale_ref[which] * update),
        )
        return carry

    lax.fori_loop(0, source.shape[0] - 2 - 2 * which, one_row, 0)


def spectral_kernel(
    normed_ref, first_ref, rest_ref, expand_from, reduce_from,
    field_ref, mask_ref, taps_ref, gain_ref, scale_ref, out_ref, ocean_ref,
    kernels_ref, arrived_ref, back_ref, wide_ref, w_hi, w_lo, f_hi, f_lo, b_hi, b_lo,
    second_ref, expand_ref, reduce_ref, expand_hi, expand_lo, reduce_hi, reduce_lo, weight_sem,
    go_send, go_recv, go_local, come_send, come_recv, come_local, swap_send, swap_recv, own_sem,
):
    count = normed_ref.shape[0]
    steps = arrived_ref.shape[0]
    groups = steps // 2
    me = lax.axis_index("lat")
    member = lax.axis_index("members")
    peers = [(k, lax.rem(me + k, count)) for k in range(1, count)]
    barrier = pltpu.get_barrier_semaphore()
    for _, peer in peers:
        pl.semaphore_signal(
            barrier, inc=1, device_id={"lat": peer}, device_id_type=pl.DeviceIdType.MESH
        )
    pl.semaphore_signal(
        barrier, inc=1, device_id={"members": 1 - member}, device_id_type=pl.DeviceIdType.MESH
    )

    def place(step):
        second = step // groups
        return member + second - 2 * member * second, pl.ds(PACK * (step % groups), PACK)

    def going(step, k, peer):
        half, span = place(step)
        return pltpu.make_async_remote_copy(
            src_ref=normed_ref.at[peer, half, span],
            dst_ref=arrived_ref.at[step, me],
            send_sem=go_send.at[step, k - 1],
            recv_sem=go_recv.at[step, k - 1],
            device_id={"lat": peer},
            device_id_type=pl.DeviceIdType.MESH,
        )

    def staying(step):
        half, span = place(step)
        return pltpu.make_async_copy(
            normed_ref.at[me, half, span], arrived_ref.at[step, me], go_local.at[step]
        )

    def coming(step, k, peer):
        half, span = place(step)
        return pltpu.make_async_remote_copy(
            src_ref=back_ref.at[step, peer],
            dst_ref=out_ref.at[me, half, span],
            send_sem=come_send.at[step, k - 1],
            recv_sem=come_recv.at[step, k - 1],
            device_id={"lat": peer},
            device_id_type=pl.DeviceIdType.MESH,
        )

    def kept(step):
        half, span = place(step)
        return pltpu.make_async_copy(
            back_ref.at[step, me], out_ref.at[me, half, span], come_local.at[step]
        )

    def held(group):
        begun = first_ref.shape[2]
        return first_ref.at[:, :, group] if group < begun else rest_ref.at[:, :, group - begun]

    def own_filter(group):
        return pltpu.make_async_copy(held(group), kernels_ref.at[group], own_sem.at[group])

    def swapped(group):
        return pltpu.make_async_remote_copy(
            src_ref=held(group),
            dst_ref=kernels_ref.at[groups + group],
            send_sem=swap_send.at[group],
            recv_sem=swap_recv.at[group],
            device_id={"members": 1 - member},
            device_id_type=pl.DeviceIdType.MESH,
        )

    pl.semaphore_wait(barrier, count)
    for step in range(steps):
        for k, peer in peers:
            going(step, k, peer).start()
        staying(step).start()
        if step < groups:
            own_filter(step).start()
            swapped(step).start()

    fetches = [
        pltpu.make_async_copy(expand_from, expand_ref, weight_sem.at[0]),
        pltpu.make_async_copy(reduce_from, reduce_ref, weight_sem.at[1]),
    ]
    for fetch in fetches:
        fetch.start()
    fill_tables(w_hi, w_lo, f_hi, f_lo, b_hi, b_lo)
    for fetch in fetches:
        fetch.wait()

    def keep_second(row, values):
        second_ref[row, 8 : 8 + values.shape[0], :] = values

    def keep_ocean(row, values):
        ocean_ref[row - 2] = values

    wide_columns = field_ref.shape[1]
    spans = (slice(8, wide_columns - 8), slice(RIM, RIM + ocean_ref.shape[1]))
    for which, source, store in ((0, field_ref, keep_second), (1, second_ref, keep_ocean)):
        expand_hi[...], expand_lo[...] = split_value(expand_ref[which])
        reduce_hi[...], reduce_lo[...] = split_value(reduce_ref[which])
        ocean_block(
            which, source, mask_ref, taps_ref, gain_ref, scale_ref,
            (expand_hi, expand_lo, reduce_hi, reduce_lo), spans[which], store,
        )

    def one_step(step, carry):
        staying(step).wait()
        for k, peer in peers:
            going(step, k, peer).wait_recv()

        for group in range(groups):

            @pl.when(step == group)
            def _():
                own_filter(group).wait()

            @pl.when(step == groups + group)
            def _():
                swapped(group).wait_recv()

        filter_group(
            arrived_ref.at[step],
            kernels_ref.at[step],
            (w_hi, w_lo, f_hi, f_lo, b_hi, b_lo),
            back_ref.at[step],
            wide_ref,
        )
        for k, peer in peers:
            coming(step, k, peer).start()
        kept(step).start()
        return carry

    lax.fori_loop(0, steps, one_step, 0)
    for group in range(groups):
        swapped(group).wait_send()
    for step in range(steps):
        kept(step).wait()
        for k, peer in peers:
            going(step, k, peer).wait_send()
            coming(step, k, peer).wait()


def spectral_step(normed, first, rest, expand, reduce_w, field, mask, taps, gain, scale):
    lat_count, halves, _, rows, width = normed.shape
    parts, groups = first.shape[1], first.shape[2] + rest.shape[2]
    height = lat_count * rows
    steps = halves * groups
    rows_out, cols_out = field.shape[0] - 4, field.shape[1] - 24
    anywhere = pl.BlockSpec(memory_space=pl.ANY)
    inside = pl.BlockSpec(memory_space=pltpu.VMEM)
    dma = pltpu.SemaphoreType.DMA
    tables = [(width, 2 * width)] * 2 + [(2 * height, 2 * height)] * 4
    return pl.pallas_call(
        spectral_kernel,
        out_shape=(
            jax.ShapeDtypeStruct(normed.shape, jnp.float32),
            jax.ShapeDtypeStruct((rows_out, cols_out, field.shape[2]), jnp.float32),
        ),
        in_specs=[anywhere] * 5 + [inside] * 5,
        out_specs=(anywhere, inside),
        scratch_shapes=[
            pltpu.VMEM((steps, lat_count, parts) + first.shape[3:], jnp.float32),
            pltpu.VMEM((steps, lat_count, PACK, rows, width), jnp.float32),
            pltpu.VMEM((steps, lat_count, PACK, rows, width), jnp.float32),
            pltpu.VMEM((PACK * height, 2 * width), jnp.float32),
            *(pltpu.VMEM(shape, jnp.bfloat16) for shape in tables),
            pltpu.VMEM(field.shape, jnp.float32),
            pltpu.VMEM(expand.shape, jnp.float32),
            pltpu.VMEM(reduce_w.shape, jnp.float32),
            pltpu.VMEM(expand.shape[1:], jnp.bfloat16),
            pltpu.VMEM(expand.shape[1:], jnp.bfloat16),
            pltpu.VMEM(reduce_w.shape[1:], jnp.bfloat16),
            pltpu.VMEM(reduce_w.shape[1:], jnp.bfloat16),
            dma((2,)),
            dma((steps, lat_count - 1)),
            dma((steps, lat_count - 1)),
            dma((steps,)),
            dma((steps, lat_count - 1)),
            dma((steps, lat_count - 1)),
            dma((steps,)),
            dma((groups,)),
            dma((groups,)),
            dma((groups,)),
        ],
        compiler_params=pltpu.CompilerParams(collective_id=1, has_side_effects=True),
        cost_estimate=pl.CostEstimate(
            flops=12 * steps * PACK * height * width * (2 * width + 2 * height),
            transcendentals=0,
            bytes_accessed=8 * normed.size + 4 * (first.size + rest.size),
        ),
    )(normed, first, rest, expand, reduce_w, field, mask, taps, gain, scale)


def exchanged(x):
    return lax.all_to_all(x, "lat", split_axis=0, concat_axis=0, tiled=True)


def summed(x, axes):
    for axis in axes:
        if lax.axis_size(axis) == 2:
            x = x + lax.ppermute(x, axis, [(0, 1), (1, 0)])
        else:
            x = lax.psum(x, axis)
    return x


def channels_divide(atmos_state, spectral_filter, ocean_rows, ocean_cols):
    channels, rows, width = atmos_state.shape
    height = spectral_filter.shape[3]
    unit = lax.axis_size("lat") * lax.axis_size("members") * PACK
    return (
        channels % unit == 0
        and lax.axis_size("members") == 2
        and rows % 8 == 0
        and width % LANES == 0
        and PACK * height == (PACK - 1) * LANES
        and spectral_filter.shape[2] % 8 == 0
        and (lax.axis_size("lat") * rows) % TABLE_ROWS == 0
        and width % TABLE_ROWS == 0
        and channels > unit
        and ocean_cols % 8 == 0
        and width >= ocean_cols
        and rows % ocean_rows == 0
        and ocean_rows >= 4
        and rows // ocean_rows >= 3
    )


def depthwise(field, taps):
    height = field.shape[1] - 2
    width = field.shape[2] - 2
    result = jnp.zeros((field.shape[0], height, width), jnp.float32)
    for row_off in range(3):
        for col_off in range(3):
            result = (
                result
                + taps[:, 3 * row_off + col_off][:, None, None]
                * field[:, row_off : row_off + height, col_off : col_off + width]
            )
    return result


def ocean_mixer(values, gain, expand, reduce_w):
    channels, height, width = values.shape
    flat = values.reshape(channels, height * width)
    centre = jnp.mean(flat, axis=0)
    spread = jnp.mean(flat * flat, axis=0) - centre * centre
    normed = (flat - centre) * lax.rsqrt(spread + EPSILON) * gain[:, None]
    hidden = jax.nn.gelu(jnp.einsum("cd,cp->dp", expand, normed, precision=PRECISE))
    update = jnp.einsum("dc,dp->cp", reduce_w, hidden, precision=PRECISE)
    return update.reshape(channels, height, width)


def by_frequencies(
    atmos_state,
    ocean_state,
    land_mask,
    spectral_filter,
    atmos_gain,
    flux_readout,
    surface_coupling,
    surface_readout,
    flux_coupling,
    to_atmos,
    to_ocean,
    depth_taps,
    block_gain,
    expand_weight,
    reduce_weight,
    layer_scale,
):
    atmos_row_source, atmos_row_weight, atmos_col_source, atmos_col_weight = to_atmos
    ocean_row_source, ocean_row_weight, ocean_col_source, ocean_col_weight = to_ocean
    atm_rows = atmos_state.shape[1]
    width_atm = atmos_state.shape[2]
    ocean_rows = ocean_state.shape[1]
    ocean_cols = ocean_state.shape[2]
    col_groups = lax.axis_size(("lon", "chan"))
    atm_cols = width_atm // col_groups
    lat_place = lax.axis_index("lat")
    col_place = lax.axis_index(("lon", "chan"))
    partial_flux = jnp.einsum("fc,chw->fhw", flux_readout, atmos_state, precision=PRECISE)
    flux_full, column_sum, square_sum = lax.psum(
        (partial_flux, jnp.sum(atmos_state, axis=0), jnp.sum(atmos_state * atmos_state, axis=0)),
        ("lon", "chan"),
    )
    centre = column_sum / CA
    spread = square_sum / CA - centre * centre
    scale = lax.rsqrt(spread + EPSILON)
    normed = (atmos_state - centre) * scale * atmos_gain[:, None, None]
    filtered = global_filter(normed, spectral_filter)
    surface = jnp.einsum("sc,chw->shw", surface_readout, ocean_state, precision=PRECISE)
    surface_rim = grid_rims(surface)
    row_map = regrid_matrix(
        atmos_row_source, atmos_row_weight, lat_place * ocean_rows - 2, ocean_rows + 4, 0
    )
    col_map = regrid_matrix(
        atmos_col_source,
        atmos_col_weight,
        col_place * ocean_cols - 2,
        ocean_cols + 4,
        ocean_cols * col_groups,
    )
    atmos_piece = apply_maps(surface_rim, row_map, col_map)
    forcing = jnp.einsum(
        "cs,shw->chw",
        surface_coupling,
        lax.all_gather(atmos_piece, ("lon", "chan"), axis=2, tiled=True),
        precision=PRECISE,
    )
    atmos_next = atmos_state + filtered + forcing
    flux_cols = lax.dynamic_slice_in_dim(flux_full, col_place * atm_cols, atm_cols, 2)
    flux_rim = grid_rims(flux_cols)
    row_back = regrid_matrix(
        ocean_row_source, ocean_row_weight, lat_place * atm_rows - 2, atm_rows + 4, 0
    )
    col_back = regrid_matrix(
        ocean_col_source, ocean_col_weight, col_place * atm_cols - 2, atm_cols + 4, width_atm
    )
    flux_ocean = apply_maps(flux_rim, row_back, col_back)
    ocean_mask = land_mask.astype(jnp.float32)
    current = ocean_mask * (
        ocean_state + jnp.einsum("cf,fhw->chw", flux_coupling, flux_ocean, precision=PRECISE)
    )
    padded_field = grid_rims(current)
    mask_padded = grid_rims(ocean_mask[None])[0]
    update = ocean_mixer(
        depthwise(padded_field, depth_taps[0]), block_gain[0], expand_weight[0], reduce_weight[0]
    )
    widened = mask_padded[1:-1, 1:-1] * (
        padded_field[:, 1:-1, 1:-1] + layer_scale[0][:, None, None] * update
    )
    update = ocean_mixer(
        depthwise(widened, depth_taps[1]), block_gain[1], expand_weight[1], reduce_weight[1]
    )
    current = ocean_mask * (widened[:, 1:-1, 1:-1] + layer_scale[1][:, None, None] * update)
    return (atmos_next, current)


def by_channels(
    atmos_state,
    ocean_state,
    land_mask,
    spectral_filter,
    atmos_gain,
    flux_readout,
    surface_coupling,
    surface_readout,
    flux_coupling,
    to_atmos,
    to_ocean,
    depth_taps,
    block_gain,
    expand_weight,
    reduce_weight,
    layer_scale,
):
    channels, atm_rows, width_atm = atmos_state.shape
    ocean_channels, ocean_rows, ocean_cols = ocean_state.shape
    fields = surface_readout.shape[0]
    fluxes = flux_readout.shape[0]
    col_groups = lax.axis_size(("lon", "chan"))
    atm_cols = width_atm // col_groups
    lat_count = lax.axis_size("lat")
    lat_place = lax.axis_index("lat")
    col_place = lax.axis_index(("lon", "chan"))
    hold = lax.optimization_barrier

    mask = land_mask.astype(jnp.float32)
    groups = channels // (lat_count * 2 * PACK)
    packed_first = pack_filter(spectral_filter, lat_count, 2, 0, 1)
    packed_first, ocean_state, atmos_state = hold((packed_first, ocean_state, atmos_state))
    kernels_first = exchanged(packed_first)
    packed_rest = pack_filter(spectral_filter, lat_count, 2, 1, groups - 1)
    up = [(i, (i + 1) % lat_count) for i in range(lat_count)]
    down = [(j, i) for i, j in up]
    partial_flux = jnp.einsum("fc,chw->fhw", flux_readout, atmos_state, precision=EXACT)
    own_rows = regrid_matrix(to_ocean[0], to_ocean[1], lat_place * atm_rows - 1, atm_rows + 1, 0)
    by_rows = jnp.einsum("jh,fhw->fjw", own_rows[:, 1:], partial_flux, precision=PRECISE)
    weight_up = own_rows[0, 0]
    closing = partial_flux[:, -1:]

    def with_mask(rows, edge):
        edge = jnp.pad(edge, ((0, 1), (0, width_atm - ocean_cols)))
        return jnp.concatenate([rows, edge[None]], axis=0)

    to_below = with_mask(jnp.concatenate([by_rows[:, -2:], closing], axis=1), mask[-2:])
    to_above = with_mask(
        jnp.concatenate([by_rows[:, :2], jnp.broadcast_to(weight_up, closing.shape)], axis=1),
        mask[:2],
    )
    rows_before = lax.ppermute(ocean_state[:, -2:], "lat", up)
    rows_after = lax.ppermute(ocean_state[:, :2], "lat", down)
    from_above = lax.ppermute(to_below, "lat", up)
    from_below = lax.ppermute(to_above, "lat", down)
    kernels_rest = exchanged(packed_rest)
    mask_above, mask_below = from_above[fluxes, :2, :ocean_cols], from_below[fluxes, :2, :ocean_cols]
    from_above, from_below = from_above[:fluxes], from_below[:fluxes]

    flux_rows = jnp.concatenate(
        [
            from_above[:, :2],
            by_rows[:, :1] + weight_up * from_above[:, 2:],
            by_rows[:, 1:],
            from_below[:, :1] + from_below[:, 2:] * closing,
            from_below[:, 1:2],
        ],
        axis=1,
    )
    sums = jnp.stack([jnp.sum(atmos_state, axis=0), jnp.sum(atmos_state * atmos_state, axis=0)])
    ext_rows = flux_rows.shape[1]
    sent = jnp.concatenate(
        [flux_rows.reshape(fluxes * ext_rows, width_atm), sums.reshape(2 * atm_rows, width_atm)],
        axis=0,
    )
    full = summed(sent, ("chan", "lon"))
    flux_full = full[: fluxes * ext_rows].reshape(fluxes, ext_rows, width_atm)
    sums_full = full[fluxes * ext_rows :].reshape(2, atm_rows, width_atm)
    centre = sums_full[0] / CA
    spread = sums_full[1] / CA - centre * centre
    scale = lax.rsqrt(spread + EPSILON)
    normed = (atmos_state - centre) * scale * atmos_gain[:, None, None]
    own = channels // (2 * lat_count)
    halves = (lat_count, 2, own)
    normed = normed.reshape(halves + (atm_rows, width_atm))

    columns = jnp.concatenate([to_ocean[2].astype(jnp.float32), to_ocean[3]], axis=1).T
    columns = jnp.pad(columns, ((0, ocean_rows), (0, 0)))[None]
    state_rows = jnp.concatenate(
        [
            jnp.concatenate([rows_before, ocean_state, rows_after], axis=1),
            jnp.concatenate([mask_above, mask, mask_below], axis=0)[None],
            columns,
        ],
        axis=0,
    )
    state_rim = padded(state_rows, ((("lon", "chan"), 2),), 2)
    surface_rim = jnp.einsum(
        "sc,chw->shw", surface_readout, state_rim[:ocean_channels], precision=EXACT
    )
    to_atmos, state_rim = hold((to_atmos, state_rim))
    row_map = regrid_matrix(
        to_atmos[0], to_atmos[1], lat_place * ocean_rows - 2, ocean_rows + 4, 0
    )
    col_map = regrid_matrix(
        to_atmos[2],
        to_atmos[3],
        col_place * ocean_cols - 2,
        ocean_cols + 4,
        ocean_cols * col_groups,
    )
    atmos_piece = apply_maps(surface_rim, row_map, col_map)
    spread_piece = lax.dynamic_update_slice_in_dim(
        jnp.zeros((fields, atm_rows, width_atm), jnp.float32), atmos_piece, col_place * atm_cols, 2
    )
    surface_atmos = summed(spread_piece, ("chan", "lon"))

    col_tables = state_rim[ocean_channels + 1]
    col_back = regrid_matrix(col_tables[:2].T, col_tables[2:4].T, 0.0, width_atm, 0)
    flux_ocean_rim = jnp.einsum("fhw,kw->fhk", flux_full, col_back, precision=PRECISE)

    mask_rim = state_rim[ocean_channels]
    padded_field = mask_rim * (
        state_rim[:ocean_channels]
        + jnp.einsum("cf,fhw->chw", flux_coupling, flux_ocean_rim, precision=PRECISE)
    )
    aside = ((0, 0), (RIM - 2, 24 - RIM - 2))
    field = jnp.pad(jnp.transpose(padded_field, (1, 2, 0)), aside + ((0, 0),))
    mask_field = jnp.pad(mask_rim, aside)[:, :, None]
    small = (jnp.transpose(depth_taps, (0, 2, 1)), block_gain[:, None], layer_scale[:, None])

    kernels_first, kernels_rest, normed, field, surface_atmos = hold(
        (kernels_first, kernels_rest, normed, field, surface_atmos)
    )
    filtered, ocean_rows_next = spectral_step(
        normed, kernels_first, kernels_rest, expand_weight, reduce_weight, field, mask_field, *small
    )
    ocean_next = jnp.transpose(ocean_rows_next, (2, 0, 1))
    by_half = atmos_state.reshape(halves + (atm_rows, width_atm))
    coupling_half = surface_coupling.reshape(halves + (fields, 1, 1))
    forcing = sum(coupling_half[:, :, :, s] * surface_atmos[s] for s in range(fields))
    atmos_next = (by_half + filtered) + forcing
    return (atmos_next.reshape(atmos_state.shape), ocean_next)


def body(
    atmos_state,
    ocean_state,
    land_mask,
    spectral_filter,
    atmos_gain,
    flux_readout,
    surface_coupling,
    surface_readout,
    flux_coupling,
    atmos_row_source,
    atmos_row_weight,
    atmos_col_source,
    atmos_col_weight,
    ocean_row_source,
    ocean_row_weight,
    ocean_col_source,
    ocean_col_weight,
    depth_taps,
    block_gain,
    expand_weight,
    reduce_weight,
    layer_scale,
):
    if channels_divide(atmos_state, spectral_filter, *ocean_state.shape[1:]):
        step = by_channels
    else:
        step = by_frequencies
    return step(
        atmos_state,
        ocean_state,
        land_mask,
        spectral_filter,
        atmos_gain,
        flux_readout,
        surface_coupling,
        surface_readout,
        flux_coupling,
        (atmos_row_source, atmos_row_weight, atmos_col_source, atmos_col_weight),
        (ocean_row_source, ocean_row_weight, ocean_col_source, ocean_col_weight),
        depth_taps,
        block_gain,
        expand_weight,
        reduce_weight,
        layer_scale,
    )


def solution(mesh):
    return jax.shard_map(
        body,
        mesh=mesh,
        in_specs=(
            P(("members", "lon", "chan"), "lat", None),
            P("members", "lat", ("lon", "chan")),
            P("lat", ("lon", "chan")),
            P(None, ("lon", "chan"), "lat", None),
            P(("lon", "chan")),
            P(None, ("lon", "chan")),
            P(("lon", "chan"), None),
            P(),
            P(),
            P("lat", None),
            P("lat", None),
            P(("lon", "chan"), None),
            P(("lon", "chan"), None),
            P("lat", None),
            P("lat", None),
            P(("lon", "chan"), None),
            P(("lon", "chan"), None),
            P(),
            P(),
            P(),
            P(),
            P(),
        ),
        out_specs=(
            P(("members", "lon", "chan"), "lat", None),
            P("members", "lat", ("lon", "chan")),
        ),
        check_vma=False,
    )
```

```python
import functools
import math

import jax
import jax.numpy as jnp
from jax import lax
from jax.experimental import pallas as pl
from jax.experimental.pallas import tpu as pltpu
from jax.sharding import PartitionSpec as P

CA = 384


EPSILON = 1e-05
PRECISE = lax.Precision.HIGH
EXACT = lax.Precision.HIGHEST
LANES = 128
PACK = 4
TABLE_ROWS = 16
RIM = 9
PACK_VMEM = 4 << 20
STEP_VMEM = 36 << 20


def padded(x, sides, width):
    for axis, dim in sides:
        count, length = (lax.axis_size(axis), x.shape[dim])
        up = [(i, (i + 1) % count) for i in range(count)]
        down = [(j, i) for i, j in up]
        last = lax.slice_in_dim(x, length - width, length, axis=dim)
        leading = lax.slice_in_dim(x, 0, width, axis=dim)
        before = lax.ppermute(last, axis, up)
        after = lax.ppermute(leading, axis, down)
        x = jnp.concatenate([before, x, after], axis=dim)
    return x


def fourier_tables(length):
    places = jnp.arange(length, dtype=jnp.int32)
    angles = (
        2.0
        * math.pi
        / length
        * jnp.mod(places[:, None] * places[None, :], length).astype(jnp.float32)
    )
    return (jnp.cos(angles), jnp.sin(angles))


def regrid_matrix(source, weight, offset, span, period):
    shares = weight / jnp.sum(weight, axis=1, keepdims=True)
    relative = source - offset
    if period > 0:
        relative = jnp.mod(relative, period)
    columns = jnp.arange(span, dtype=relative.dtype)[None, :]
    return shares[:, 0:1] * (relative[:, 0:1] == columns).astype(jnp.float32) + shares[:, 1:2] * (
        relative[:, 1:2] == columns
    ).astype(jnp.float32)


def apply_maps(field, row_map, col_map):
    by_rows = jnp.einsum("jh,shw->sjw", row_map, field, precision=PRECISE)
    return jnp.einsum("sjw,kw->sjk", by_rows, col_map, precision=PRECISE)


def grid_rims(field):
    return padded(field, (("lat", 1), (("lon", "chan"), 2)), 2)


def along_last(field, table):
    return jnp.einsum("ckh,hm->ckm", field, table, precision=PRECISE)


def global_filter(normed, spectral_filter):
    width_len = normed.shape[2]
    height_len = spectral_filter.shape[3]
    cos_w, sin_w = fourier_tables(width_len)
    cos_h, sin_h = fourier_tables(height_len)
    real_w = jnp.einsum("chn,nk->ckh", normed, cos_w, precision=PRECISE)
    imag_w = -jnp.einsum("chn,nk->ckh", normed, sin_w, precision=PRECISE)
    real_w, imag_w = (
        lax.all_to_all(real_w, "lat", split_axis=1, concat_axis=2, tiled=True),
        lax.all_to_all(imag_w, "lat", split_axis=1, concat_axis=2, tiled=True),
    )
    real_s = along_last(real_w, cos_h) + along_last(imag_w, sin_h)
    imag_s = along_last(imag_w, cos_h) - along_last(real_w, sin_h)
    kern_real = spectral_filter[0]
    kern_imag = spectral_filter[1]
    real_f = kern_real * real_s - kern_imag * imag_s
    imag_f = kern_real * imag_s + kern_imag * real_s
    real_b = (along_last(real_f, cos_h) - along_last(imag_f, sin_h)) / height_len
    imag_b = (along_last(imag_f, cos_h) + along_last(real_f, sin_h)) / height_len
    real_b, imag_b = (
        lax.all_to_all(real_b, "lat", split_axis=2, concat_axis=1, tiled=True),
        lax.all_to_all(imag_b, "lat", split_axis=2, concat_axis=1, tiled=True),
    )
    back = jnp.einsum("ckh,kn->chn", real_b, cos_w, precision=PRECISE) - jnp.einsum(
        "ckh,kn->chn", imag_b, sin_w, precision=PRECISE
    )
    return back / width_len


def split_value(x):
    high = x.astype(jnp.bfloat16)
    return high, (x - high.astype(jnp.float32)).astype(jnp.bfloat16)


def wave(rows, columns, length):
    steps = lax.rem(rows * columns, length)
    angles = (2.0 * math.pi / length) * steps.astype(jnp.float32)
    return jnp.cos(angles), jnp.sin(angles)


def fill_tables(w_hi, w_lo, f_hi, f_lo, b_hi, b_lo):
    width, height = w_hi.shape[0], f_hi.shape[0] // 2

    def places(block, columns):
        shape = (TABLE_ROWS, columns)
        rows = lax.broadcasted_iota(jnp.int32, shape, 0) + block * TABLE_ROWS
        return rows, lax.broadcasted_iota(jnp.int32, shape, 1)

    def span(block):
        return pl.ds(pl.multiple_of(block * TABLE_ROWS, TABLE_ROWS), TABLE_ROWS)

    def along_width(block, carry):
        cos_w, sin_w = wave(*places(block, width), width)
        w_hi[span(block), :width], w_lo[span(block), :width] = split_value(cos_w)
        w_hi[span(block), width:], w_lo[span(block), width:] = split_value(-sin_w)
        return carry

    def along_height(block, carry):
        rows, columns = places(block, 2 * height)
        lower, right = rows >= height, columns >= height
        cos_h, sin_h = wave(
            jnp.where(lower, rows - height, rows), jnp.where(right, columns - height, columns), height
        )
        level = lower == right
        forward = jnp.where(level, cos_h, jnp.where(right, sin_h, -sin_h))
        inverse = jnp.where(level, cos_h, jnp.where(right, -sin_h, sin_h)) / (height * width)
        f_hi[span(block), :], f_lo[span(block), :] = split_value(forward)
        b_hi[span(block), :], b_lo[span(block), :] = split_value(inverse)
        return carry

    lax.fori_loop(0, width // TABLE_ROWS, along_width, 0)
    lax.fori_loop(0, 2 * height // TABLE_ROWS, along_height, 0)


def product(left, right):
    dot = functools.partial(jnp.dot, preferred_element_type=jnp.float32)
    return dot(left[0], right[0]) + (dot(left[0], right[1]) + dot(left[1], right[0]))


def product_transposed(left, right):
    dot = functools.partial(
        lax.dot_general,
        dimension_numbers=(((1,), (1,)), ((), ())),
        preferred_element_type=jnp.float32,
    )
    return dot(left[0], right[0]) + (dot(left[0], right[1]) + dot(left[1], right[0]))


def pack_kernel(member_ref, filter_ref, packed_ref):
    del member_ref
    piece = LANES // PACK
    for part in range(filter_ref.shape[0]):
        last = filter_ref[part, 0, 0, 0, PACK - 1]
        for j in range(PACK - 1):
            packed_ref[0, part, 0, j] = jnp.concatenate(
                [filter_ref[part, 0, 0, 0, j], last[:, piece * j : piece * (j + 1)]],
                axis=1,
            )


def pack_filter(spectral_filter, lat_count, members, first, count):
    parts, channels, freqs, height_len = spectral_filter.shape
    groups = channels // (lat_count * members * PACK)
    member = lax.axis_index("members").astype(jnp.int32).reshape(1)
    split = spectral_filter.reshape(parts, lat_count, members, groups, PACK, freqs, height_len)
    return pl.pallas_call(
        pack_kernel,
        out_shape=jax.ShapeDtypeStruct(
            (lat_count, parts, count, PACK - 1, freqs, LANES), jnp.float32
        ),
        grid_spec=pltpu.PrefetchScalarGridSpec(
            num_scalar_prefetch=1,
            grid=(lat_count, count),
            in_specs=[
                pl.BlockSpec(
                    (parts, 1, 1, 1, PACK, freqs, height_len),
                    lambda i, g, m: (0, i, m[0], g + first, 0, 0, 0),
                )
            ],
            out_specs=pl.BlockSpec(
                (1, parts, 1, PACK - 1, freqs, LANES), lambda i, g, m: (i, 0, g, 0, 0, 0)
            ),
        ),
        compiler_params=pltpu.CompilerParams(vmem_limit_bytes=PACK_VMEM),
        cost_estimate=pl.CostEstimate(
            flops=0,
            transcendentals=0,
            bytes_accessed=6 * spectral_filter.size * count // groups,
        ),
    )(member, split)


def filter_group(x_ref, filter_ref, tables, out_ref, wide_ref):
    blocks, _, block_rows, width = x_ref.shape
    height = blocks * block_rows
    w_hi, w_lo, f_hi, f_lo, b_hi, b_lo = tables
    table_w = (w_hi[...], w_lo[...])
    forward = (f_hi[...], f_lo[...])
    inverse = (b_hi[...], b_lo[...])
    rows = jnp.concatenate([x_ref[:, j].reshape(height, width) for j in range(PACK)], axis=0)
    spectra = product(split_value(rows), table_w)
    packed = [
        [filter_ref[:, part, j].reshape(width, LANES).T for j in range(PACK - 1)]
        for part in range(2)
    ]
    kernels = [
        [p[:height] for p in of_part] + [jnp.concatenate([p[height:] for p in of_part], axis=0)]
        for of_part in packed
    ]
    for j in range(PACK):
        own = spectra[height * j : height * (j + 1)]
        stacked = jnp.concatenate([own[:, :width], own[:, width:]], axis=0)
        full = product(forward, split_value(stacked))
        real_s, imag_s = full[:height], full[height:]
        real_k, imag_k = kernels[0][j], kernels[1][j]
        filtered = jnp.concatenate(
            [real_k * real_s - imag_k * imag_s, real_k * imag_s + imag_k * real_s], axis=0
        )
        back = product(inverse, split_value(filtered))
        wide_ref[height * j : height * (j + 1), :width] = back[:height]
        wide_ref[height * j : height * (j + 1), width:] = back[height:]
    wide = split_value(wide_ref[...])
    result = product(
        (wide[0][:, :width], wide[1][:, :width]), (table_w[0][:, :width], table_w[1][:, :width])
    ) + product(
        (wide[0][:, width:], wide[1][:, width:]), (table_w[0][:, width:], table_w[1][:, width:])
    )
    for j in range(PACK):
        own = result[height * j : height * (j + 1)]
        out_ref[:, j] = own.reshape(blocks, block_rows, width)


def ocean_block(which, source, mask_ref, taps_ref, gain_ref, scale_ref, weights, span, store):
    channels = source.shape[2]
    columns = span.stop - span.start
    expand_hi, expand_lo, reduce_hi, reduce_lo = weights

    def one_row(index, carry):
        row = index + 1 + which
        conv = jnp.zeros((columns, channels), jnp.float32)
        for row_off in range(3):
            for col_off in range(3):
                tap = 3 * row_off + col_off
                begin = span.start + col_off - 1
                conv = conv + taps_ref[which, tap : tap + 1, :] * (
                    source[row + row_off - 1, begin : begin + columns, :]
                )
        centre = jnp.sum(conv, axis=1, keepdims=True) / channels
        spread = jnp.sum(conv * conv, axis=1, keepdims=True) / channels - centre * centre
        normed = (conv - centre) * lax.rsqrt(spread + EPSILON) * gain_ref[which : which + 1, :]
        hidden = jax.nn.gelu(product(split_value(normed), (expand_hi[...], expand_lo[...])))
        update = product_transposed(split_value(hidden), (reduce_hi[...], reduce_lo[...]))
        store(
            row,
            mask_ref[row, span, :] * (source[row, span, :] + scale_ref[which : which + 1, :] * update),
        )
        return carry

    lax.fori_loop(0, source.shape[0] - 2 - 2 * which, one_row, 0)


def spectral_kernel(
    normed_ref, first_ref, rest_ref, expand_from, reduce_from,
    field_ref, mask_ref, taps_ref, gain_ref, scale_ref, out_ref, ocean_ref,
    kernels_ref, arrived_ref, back_ref, wide_ref, w_hi, w_lo, f_hi, f_lo, b_hi, b_lo,
    second_ref, expand_ref, reduce_ref, expand_hi, expand_lo, reduce_hi, reduce_lo, weight_sem,
    go_send, go_recv, go_local, come_send, come_recv, come_local, swap_send, swap_recv, own_sem,
):
    count = normed_ref.shape[0]
    steps = arrived_ref.shape[0]
    groups = steps // 2
    me = lax.axis_index("lat")
    member = lax.axis_index("members")
    peers = [(k, lax.rem(me + k, count)) for k in range(1, count)]
    barrier = pltpu.get_barrier_semaphore()
    for _, peer in peers:
        pl.semaphore_signal(
            barrier, inc=1, device_id={"lat": peer}, device_id_type=pl.DeviceIdType.MESH
        )
    pl.semaphore_signal(
        barrier, inc=1, device_id={"members": 1 - member}, device_id_type=pl.DeviceIdType.MESH
    )

    def place(step):
        second = step // groups
        return member + second - 2 * member * second, pl.ds(PACK * (step % groups), PACK)

    def going(step, k, peer):
        half, span = place(step)
        return pltpu.make_async_remote_copy(
            src_ref=normed_ref.at[peer, half, span],
            dst_ref=arrived_ref.at[step, me],
            send_sem=go_send.at[step, k - 1],
            recv_sem=go_recv.at[step, k - 1],
            device_id={"lat": peer},
            device_id_type=pl.DeviceIdType.MESH,
        )

    def staying(step):
        half, span = place(step)
        return pltpu.make_async_copy(
            normed_ref.at[me, half, span], arrived_ref.at[step, me], go_local.at[step]
        )

    def coming(step, k, peer):
        half, span = place(step)
        return pltpu.make_async_remote_copy(
            src_ref=back_ref.at[step, peer],
            dst_ref=out_ref.at[me, half, span],
            send_sem=come_send.at[step, k - 1],
            recv_sem=come_recv.at[step, k - 1],
            device_id={"lat": peer},
            device_id_type=pl.DeviceIdType.MESH,
        )

    def kept(step):
        half, span = place(step)
        return pltpu.make_async_copy(
            back_ref.at[step, me], out_ref.at[me, half, span], come_local.at[step]
        )

    def held(group):
        begun = first_ref.shape[2]
        return first_ref.at[:, :, group] if group < begun else rest_ref.at[:, :, group - begun]

    def own_filter(group):
        return pltpu.make_async_copy(held(group), kernels_ref.at[group], own_sem.at[group])

    def swapped(group):
        return pltpu.make_async_remote_copy(
            src_ref=held(group),
            dst_ref=kernels_ref.at[groups + group],
            send_sem=swap_send.at[group],
            recv_sem=swap_recv.at[group],
            device_id={"members": 1 - member},
            device_id_type=pl.DeviceIdType.MESH,
        )

    pl.semaphore_wait(barrier, count)
    for step in range(steps):
        for k, peer in peers:
            going(step, k, peer).start()
        staying(step).start()
        if step < groups:
            own_filter(step).start()
            swapped(step).start()

    fetches = [
        pltpu.make_async_copy(expand_from, expand_ref, weight_sem.at[0]),
        pltpu.make_async_copy(reduce_from, reduce_ref, weight_sem.at[1]),
    ]
    for fetch in fetches:
        fetch.start()
    fill_tables(w_hi, w_lo, f_hi, f_lo, b_hi, b_lo)
    for fetch in fetches:
        fetch.wait()

    def keep_second(row, values):
        second_ref[row, 8 : 8 + values.shape[0], :] = values

    def keep_ocean(row, values):
        ocean_ref[row - 2] = values

    wide_columns = field_ref.shape[1]
    spans = (slice(8, wide_columns - 8), slice(RIM, RIM + ocean_ref.shape[1]))
    for which, source, store in ((0, field_ref, keep_second), (1, second_ref, keep_ocean)):
        expand_hi[...], expand_lo[...] = split_value(expand_ref[which])
        reduce_hi[...], reduce_lo[...] = split_value(reduce_ref[which])
        ocean_block(
            which, source, mask_ref, taps_ref, gain_ref, scale_ref,
            (expand_hi, expand_lo, reduce_hi, reduce_lo), spans[which], store,
        )

    def one_step(step, carry):
        staying(step).wait()
        for k, peer in peers:
            going(step, k, peer).wait_recv()

        for group in range(groups):

            @pl.when(step == group)
            def _():
                own_filter(group).wait()

            @pl.when(step == groups + group)
            def _():
                swapped(group).wait_recv()

        filter_group(
            arrived_ref.at[step],
            kernels_ref.at[step],
            (w_hi, w_lo, f_hi, f_lo, b_hi, b_lo),
            back_ref.at[step],
            wide_ref,
        )
        for k, peer in peers:
            coming(step, k, peer).start()
        kept(step).start()
        return carry

    lax.fori_loop(0, steps, one_step, 0)
    for group in range(groups):
        swapped(group).wait_send()
    for step in range(steps):
        kept(step).wait()
        for k, peer in peers:
            going(step, k, peer).wait_send()
            coming(step, k, peer).wait()


def spectral_step(normed, first, rest, expand, reduce_w, field, mask, taps, gain, scale):
    lat_count, halves, _, rows, width = normed.shape
    parts, groups = first.shape[1], first.shape[2] + rest.shape[2]
    height = lat_count * rows
    steps = halves * groups
    rows_out, cols_out = field.shape[0] - 4, field.shape[1] - 24
    anywhere = pl.BlockSpec(memory_space=pl.ANY)
    inside = pl.BlockSpec(memory_space=pltpu.VMEM)
    dma = pltpu.SemaphoreType.DMA
    tables = [(width, 2 * width)] * 2 + [(2 * height, 2 * height)] * 4
    return pl.pallas_call(
        spectral_kernel,
        out_shape=(
            jax.ShapeDtypeStruct(normed.shape, jnp.float32),
            jax.ShapeDtypeStruct((rows_out, cols_out, field.shape[2]), jnp.float32),
        ),
        in_specs=[anywhere] * 5 + [inside] * 5,
        out_specs=(anywhere, inside),
        scratch_shapes=[
            pltpu.VMEM((steps, lat_count, parts) + first.shape[3:], jnp.float32),
            pltpu.VMEM((steps, lat_count, PACK, rows, width), jnp.float32),
            pltpu.VMEM((steps, lat_count, PACK, rows, width), jnp.float32),
            pltpu.VMEM((PACK * height, 2 * width), jnp.float32),
            *(pltpu.VMEM(shape, jnp.bfloat16) for shape in tables),
            pltpu.VMEM(field.shape, jnp.float32),
            pltpu.VMEM(expand.shape, jnp.float32),
            pltpu.VMEM(reduce_w.shape, jnp.float32),
            pltpu.VMEM(expand.shape[1:], jnp.bfloat16),
            pltpu.VMEM(expand.shape[1:], jnp.bfloat16),
            pltpu.VMEM(reduce_w.shape[1:], jnp.bfloat16),
            pltpu.VMEM(reduce_w.shape[1:], jnp.bfloat16),
            dma((2,)),
            dma((steps, lat_count - 1)),
            dma((steps, lat_count - 1)),
            dma((steps,)),
            dma((steps, lat_count - 1)),
            dma((steps, lat_count - 1)),
            dma((steps,)),
            dma((groups,)),
            dma((groups,)),
            dma((groups,)),
        ],
        compiler_params=pltpu.CompilerParams(
            collective_id=1, has_side_effects=True, vmem_limit_bytes=STEP_VMEM
        ),
        cost_estimate=pl.CostEstimate(
            flops=12 * steps * PACK * height * width * (2 * width + 2 * height),
            transcendentals=0,
            bytes_accessed=8 * normed.size + 4 * (first.size + rest.size),
        ),
    )(normed, first, rest, expand, reduce_w, field, mask, taps, gain, scale)


def exchanged(x):
    return lax.all_to_all(x, "lat", split_axis=0, concat_axis=0, tiled=True)


def summed(x, axes):
    for axis in axes:
        if lax.axis_size(axis) == 2:
            x = x + lax.ppermute(x, axis, [(0, 1), (1, 0)])
        else:
            x = lax.psum(x, axis)
    return x


def channels_divide(atmos_state, spectral_filter, ocean_rows, ocean_cols):
    channels, rows, width = atmos_state.shape
    height = spectral_filter.shape[3]
    unit = lax.axis_size("lat") * lax.axis_size("members") * PACK
    return (
        channels % unit == 0
        and lax.axis_size("members") == 2
        and rows % 8 == 0
        and width % LANES == 0
        and PACK * height == (PACK - 1) * LANES
        and spectral_filter.shape[2] % 8 == 0
        and (lax.axis_size("lat") * rows) % TABLE_ROWS == 0
        and width % TABLE_ROWS == 0
        and channels > unit
        and ocean_cols % 8 == 0
        and width >= ocean_cols
        and rows % ocean_rows == 0
        and ocean_rows >= 4
        and rows // ocean_rows >= 3
    )


def depthwise(field, taps):
    height = field.shape[1] - 2
    width = field.shape[2] - 2
    result = jnp.zeros((field.shape[0], height, width), jnp.float32)
    for row_off in range(3):
        for col_off in range(3):
            result = (
                result
                + taps[:, 3 * row_off + col_off][:, None, None]
                * field[:, row_off : row_off + height, col_off : col_off + width]
            )
    return result


def ocean_mixer(values, gain, expand, reduce_w):
    channels, height, width = values.shape
    flat = values.reshape(channels, height * width)
    centre = jnp.mean(flat, axis=0)
    spread = jnp.mean(flat * flat, axis=0) - centre * centre
    normed = (flat - centre) * lax.rsqrt(spread + EPSILON) * gain[:, None]
    hidden = jax.nn.gelu(jnp.einsum("cd,cp->dp", expand, normed, precision=PRECISE))
    update = jnp.einsum("dc,dp->cp", reduce_w, hidden, precision=PRECISE)
    return update.reshape(channels, height, width)


def by_frequencies(
    atmos_state,
    ocean_state,
    land_mask,
    spectral_filter,
    atmos_gain,
    flux_readout,
    surface_coupling,
    surface_readout,
    flux_coupling,
    to_atmos,
    to_ocean,
    depth_taps,
    block_gain,
    expand_weight,
    reduce_weight,
    layer_scale,
):
    atmos_row_source, atmos_row_weight, atmos_col_source, atmos_col_weight = to_atmos
    ocean_row_source, ocean_row_weight, ocean_col_source, ocean_col_weight = to_ocean
    atm_rows = atmos_state.shape[1]
    width_atm = atmos_state.shape[2]
    ocean_rows = ocean_state.shape[1]
    ocean_cols = ocean_state.shape[2]
    col_groups = lax.axis_size(("lon", "chan"))
    atm_cols = width_atm // col_groups
    lat_place = lax.axis_index("lat")
    col_place = lax.axis_index(("lon", "chan"))
    partial_flux = jnp.einsum("fc,chw->fhw", flux_readout, atmos_state, precision=PRECISE)
    flux_full, column_sum, square_sum = lax.psum(
        (partial_flux, jnp.sum(atmos_state, axis=0), jnp.sum(atmos_state * atmos_state, axis=0)),
        ("lon", "chan"),
    )
    centre = column_sum / CA
    spread = square_sum / CA - centre * centre
    scale = lax.rsqrt(spread + EPSILON)
    normed = (atmos_state - centre) * scale * atmos_gain[:, None, None]
    filtered = global_filter(normed, spectral_filter)
    surface = jnp.einsum("sc,chw->shw", surface_readout, ocean_state, precision=PRECISE)
    surface_rim = grid_rims(surface)
    row_map = regrid_matrix(
        atmos_row_source, atmos_row_weight, lat_place * ocean_rows - 2, ocean_rows + 4, 0
    )
    col_map = regrid_matrix(
        atmos_col_source,
        atmos_col_weight,
        col_place * ocean_cols - 2,
        ocean_cols + 4,
        ocean_cols * col_groups,
    )
    atmos_piece = apply_maps(surface_rim, row_map, col_map)
    forcing = jnp.einsum(
        "cs,shw->chw",
        surface_coupling,
        lax.all_gather(atmos_piece, ("lon", "chan"), axis=2, tiled=True),
        precision=PRECISE,
    )
    atmos_next = atmos_state + filtered + forcing
    flux_cols = lax.dynamic_slice_in_dim(flux_full, col_place * atm_cols, atm_cols, 2)
    flux_rim = grid_rims(flux_cols)
    row_back = regrid_matrix(
        ocean_row_source, ocean_row_weight, lat_place * atm_rows - 2, atm_rows + 4, 0
    )
    col_back = regrid_matrix(
        ocean_col_source, ocean_col_weight, col_place * atm_cols - 2, atm_cols + 4, width_atm
    )
    flux_ocean = apply_maps(flux_rim, row_back, col_back)
    ocean_mask = land_mask.astype(jnp.float32)
    current = ocean_mask * (
        ocean_state + jnp.einsum("cf,fhw->chw", flux_coupling, flux_ocean, precision=PRECISE)
    )
    padded_field = grid_rims(current)
    mask_padded = grid_rims(ocean_mask[None])[0]
    update = ocean_mixer(
        depthwise(padded_field, depth_taps[0]), block_gain[0], expand_weight[0], reduce_weight[0]
    )
    widened = mask_padded[1:-1, 1:-1] * (
        padded_field[:, 1:-1, 1:-1] + layer_scale[0][:, None, None] * update
    )
    update = ocean_mixer(
        depthwise(widened, depth_taps[1]), block_gain[1], expand_weight[1], reduce_weight[1]
    )
    current = ocean_mask * (widened[:, 1:-1, 1:-1] + layer_scale[1][:, None, None] * update)
    return (atmos_next, current)


def by_channels(
    atmos_state,
    ocean_state,
    land_mask,
    spectral_filter,
    atmos_gain,
    flux_readout,
    surface_coupling,
    surface_readout,
    flux_coupling,
    to_atmos,
    to_ocean,
    depth_taps,
    block_gain,
    expand_weight,
    reduce_weight,
    layer_scale,
):
    channels, atm_rows, width_atm = atmos_state.shape
    ocean_channels, ocean_rows, ocean_cols = ocean_state.shape
    fields = surface_readout.shape[0]
    fluxes = flux_readout.shape[0]
    col_groups = lax.axis_size(("lon", "chan"))
    atm_cols = width_atm // col_groups
    lat_count = lax.axis_size("lat")
    lat_place = lax.axis_index("lat")
    col_place = lax.axis_index(("lon", "chan"))
    hold = lax.optimization_barrier

    mask = land_mask.astype(jnp.float32)
    groups = channels // (lat_count * 2 * PACK)
    packed_first = pack_filter(spectral_filter, lat_count, 2, 0, 1)
    packed_first, ocean_state, atmos_state = hold((packed_first, ocean_state, atmos_state))
    kernels_first = exchanged(packed_first)
    packed_rest = pack_filter(spectral_filter, lat_count, 2, 1, groups - 1)
    packed_rest, ocean_state, flux_readout = hold((packed_rest, ocean_state, flux_readout))
    up = [(i, (i + 1) % lat_count) for i in range(lat_count)]
    down = [(j, i) for i, j in up]
    partial_flux = jnp.einsum("fc,chw->fhw", flux_readout, atmos_state, precision=EXACT)
    own_rows = regrid_matrix(to_ocean[0], to_ocean[1], lat_place * atm_rows - 1, atm_rows + 1, 0)
    by_rows = jnp.einsum("jh,fhw->fjw", own_rows[:, 1:], partial_flux, precision=PRECISE)
    weight_up = own_rows[0, 0]
    closing = partial_flux[:, -1:]

    def with_mask(rows, edge):
        edge = jnp.pad(edge, ((0, 1), (0, width_atm - ocean_cols)))
        return jnp.concatenate([rows, edge[None]], axis=0)

    to_below = with_mask(jnp.concatenate([by_rows[:, -2:], closing], axis=1), mask[-2:])
    to_above = with_mask(
        jnp.concatenate([by_rows[:, :2], jnp.broadcast_to(weight_up, closing.shape)], axis=1),
        mask[:2],
    )
    to_below, to_above, rows_last, rows_first = hold(
        (to_below, to_above, ocean_state[:, -2:], ocean_state[:, :2])
    )
    rows_before = lax.ppermute(rows_last, "lat", up)
    rows_after = lax.ppermute(rows_first, "lat", down)
    from_above = lax.ppermute(to_below, "lat", up)
    from_below = lax.ppermute(to_above, "lat", down)
    kernels_rest = exchanged(packed_rest)
    mask_above, mask_below = from_above[fluxes, :2, :ocean_cols], from_below[fluxes, :2, :ocean_cols]
    from_above, from_below = from_above[:fluxes], from_below[:fluxes]

    flux_rows = jnp.concatenate(
        [
            from_above[:, :2],
            by_rows[:, :1] + weight_up * from_above[:, 2:],
            by_rows[:, 1:],
            from_below[:, :1] + from_below[:, 2:] * closing,
            from_below[:, 1:2],
        ],
        axis=1,
    )
    sums = jnp.stack([jnp.sum(atmos_state, axis=0), jnp.sum(atmos_state * atmos_state, axis=0)])
    ext_rows = flux_rows.shape[1]
    sent = jnp.concatenate(
        [flux_rows.reshape(fluxes * ext_rows, width_atm), sums.reshape(2 * atm_rows, width_atm)],
        axis=0,
    )
    full = summed(sent, ("chan", "lon"))
    flux_full = full[: fluxes * ext_rows].reshape(fluxes, ext_rows, width_atm)
    sums_full = full[fluxes * ext_rows :].reshape(2, atm_rows, width_atm)
    centre = sums_full[0] / CA
    spread = sums_full[1] / CA - centre * centre
    scale = lax.rsqrt(spread + EPSILON)
    normed = (atmos_state - centre) * scale * atmos_gain[:, None, None]
    own = channels // (2 * lat_count)
    halves = (lat_count, 2, own)
    normed = normed.reshape(halves + (atm_rows, width_atm))

    columns = jnp.concatenate([to_ocean[2].astype(jnp.float32), to_ocean[3]], axis=1).T
    columns = jnp.pad(columns, ((0, ocean_rows), (0, 0)))[None]
    state_rows = jnp.concatenate(
        [
            jnp.concatenate([rows_before, ocean_state, rows_after], axis=1),
            jnp.concatenate([mask_above, mask, mask_below], axis=0)[None],
            columns,
        ],
        axis=0,
    )
    state_rim = padded(state_rows, ((("lon", "chan"), 2),), 2)
    surface_rim = jnp.einsum(
        "sc,chw->shw", surface_readout, state_rim[:ocean_channels], precision=EXACT
    )
    to_atmos, state_rim = hold((to_atmos, state_rim))
    row_map = regrid_matrix(
        to_atmos[0], to_atmos[1], lat_place * ocean_rows - 2, ocean_rows + 4, 0
    )
    col_map = regrid_matrix(
        to_atmos[2],
        to_atmos[3],
        col_place * ocean_cols - 2,
        ocean_cols + 4,
        ocean_cols * col_groups,
    )
    atmos_piece = apply_maps(surface_rim, row_map, col_map)
    spread_piece = lax.dynamic_update_slice_in_dim(
        jnp.zeros((fields, atm_rows, width_atm), jnp.float32), atmos_piece, col_place * atm_cols, 2
    )
    surface_atmos = summed(spread_piece, ("chan", "lon"))

    col_tables = state_rim[ocean_channels + 1]
    col_back = regrid_matrix(col_tables[:2].T, col_tables[2:4].T, 0.0, width_atm, 0)
    flux_ocean_rim = jnp.einsum("fhw,kw->fhk", flux_full, col_back, precision=PRECISE)

    mask_rim = state_rim[ocean_channels]
    padded_field = mask_rim * (
        state_rim[:ocean_channels]
        + jnp.einsum("cf,fhw->chw", flux_coupling, flux_ocean_rim, precision=PRECISE)
    )
    aside = ((0, 0), (RIM - 2, 24 - RIM - 2))
    field = jnp.pad(jnp.transpose(padded_field, (1, 2, 0)), aside + ((0, 0),))
    mask_field = jnp.pad(mask_rim, aside)[:, :, None]
    reduce_flat = jnp.swapaxes(reduce_weight, 1, 2)
    small = (jnp.transpose(depth_taps, (0, 2, 1)), block_gain, layer_scale)

    kernels_first, kernels_rest, normed, field, surface_atmos = hold(
        (kernels_first, kernels_rest, normed, field, surface_atmos)
    )
    filtered, ocean_rows_next = spectral_step(
        normed, kernels_first, kernels_rest, expand_weight, reduce_flat, field, mask_field, *small
    )
    ocean_next = jnp.transpose(ocean_rows_next, (2, 0, 1))
    by_half = atmos_state.reshape(halves + (atm_rows, width_atm))
    coupling_half = surface_coupling.reshape(halves + (fields, 1, 1))
    forcing = sum(coupling_half[:, :, :, s] * surface_atmos[s] for s in range(fields))
    atmos_next = (by_half + filtered) + forcing
    return (atmos_next.reshape(atmos_state.shape), ocean_next)


def body(
    atmos_state,
    ocean_state,
    land_mask,
    spectral_filter,
    atmos_gain,
    flux_readout,
    surface_coupling,
    surface_readout,
    flux_coupling,
    atmos_row_source,
    atmos_row_weight,
    atmos_col_source,
    atmos_col_weight,
    ocean_row_source,
    ocean_row_weight,
    ocean_col_source,
    ocean_col_weight,
    depth_taps,
    block_gain,
    expand_weight,
    reduce_weight,
    layer_scale,
):
    if channels_divide(atmos_state, spectral_filter, *ocean_state.shape[1:]):
        step = by_channels
    else:
        step = by_frequencies
    return step(
        atmos_state,
        ocean_state,
        land_mask,
        spectral_filter,
        atmos_gain,
        flux_readout,
        surface_coupling,
        surface_readout,
        flux_coupling,
        (atmos_row_source, atmos_row_weight, atmos_col_source, atmos_col_weight),
        (ocean_row_source, ocean_row_weight, ocean_col_source, ocean_col_weight),
        depth_taps,
        block_gain,
        expand_weight,
        reduce_weight,
        layer_scale,
    )


def solution(mesh):
    return jax.shard_map(
        body,
        mesh=mesh,
        in_specs=(
            P(("members", "lon", "chan"), "lat", None),
            P("members", "lat", ("lon", "chan")),
            P("lat", ("lon", "chan")),
            P(None, ("lon", "chan"), "lat", None),
            P(("lon", "chan")),
            P(None, ("lon", "chan")),
            P(("lon", "chan"), None),
            P(),
            P(),
            P("lat", None),
            P("lat", None),
            P(("lon", "chan"), None),
            P(("lon", "chan"), None),
            P("lat", None),
            P("lat", None),
            P(("lon", "chan"), None),
            P(("lon", "chan"), None),
            P(),
            P(),
            P(),
            P(),
            P(),
        ),
        out_specs=(
            P(("members", "lon", "chan"), "lat", None),
            P("members", "lat", ("lon", "chan")),
        ),
        check_vma=False,
    )
```
